32 devices in a mesh: tm: 4 (over y, core), chan: 8 (over z, x).
Axes of the slice: x: 2, y: 2, z: 4, core: 2. Of those that a mesh axis runs over, the one named last changes fastest.
Arguments:
- recordings: float32 [4, 256, 8, 512], P('tm', None, 'chan')
- gap_start: int32 [4, 256, 8], P('tm', None, 'chan'), may hold values from 0 to 511
- dropout_extent: int32 [4, 256, 8], P('tm', None, 'chan'), may hold values from 0 to 256
- filter_taps: float32 [128], replicated, may hold values from -0.5 to 0.5
- source_channel: int32 [32], P('chan'), may hold values from 0 to 255
- receiver_block: int32 [32], P('chan'), may hold values from 0 to 3
Outputs:
- stacks: float32 [128, 32, 1024], P('tm', 'chan')
The draws below stay inside these ranges and needn't reach their ends.
All inputs are finite; a program needn't handle non-finite values.
Results may differ from the reference program's by a relative error of at most 0.0031.
Values may be sent and summed in bfloat16 or wider, within the bound.
No kernel may reach another device: no remote copies, remote signals or barrier semaphores. Data moves between devices by JAX's collectives and lax.ppermute only.
A program may use at most 64 MiB of HBM per device.

```python
import math
import jax
import jax.numpy as jnp
from jax import lax

BLOCK = 128
BLOCKS_DEV = 2
FRAME_READINGS = 512
TAPS = 128
MAX_LAG = 512
PAIR_DEV = 4
ROUNDS = 256
UNITS = 8
RECORD_INTERVALS = 4
PAIRS = 32


def draw_recordings(key, part):
    full_shape = (RECORD_INTERVALS, ROUNDS, UNITS, FRAME_READINGS)
    noise_key, line_seed_handle, trace_stochastic_seed = jax.random.split(key, 3)
    row_scale = jnp.exp(jax.random.uniform(line_seed_handle, (RECORD_INTERVALS, ROUNDS, UNITS, 1), jnp.float32, 0.0, math.log(10.0)))
    noise_draw = jax.random.normal(noise_key, full_shape, jnp.float32)
    trace_amplitude_multiplier = jnp.exp(jax.random.uniform(trace_stochastic_seed, (RECORD_INTERVALS, 1, 1, FRAME_READINGS), jnp.float32, 0.0, math.log(10.0)))
    return noise_draw * row_scale * trace_amplitude_multiplier


def set_ends(values, stream_key, smallest, top_value):
    extent = values.shape
    spot = [jax.random.randint(jax.random.fold_in(stream_key, axis), (), 0, extent[axis]) for axis in range(len(extent))]
    values = values.at[tuple(spot)].set(smallest)
    longest = extent.index(max(extent))
    spot[longest] = (spot[longest] + 1) % extent[longest]
    return values.at[tuple(spot)].set(top_value)


def scatter_about(key, shape, deviation, limit, kind=jnp.bfloat16):
    return jnp.clip(deviation * jax.random.normal(key, shape, jnp.float32), -limit, limit).astype(kind)


def setup_inputs(seed: int = 0) -> dict:
    streams_of = jax.random.split(jax.random.key(seed), 7)
    return {
        "recordings": draw_recordings(jax.random.fold_in(streams_of[6], 71), 0),
        "gap_start": set_ends(jax.random.randint(streams_of[1], (RECORD_INTERVALS, ROUNDS, UNITS), 0, FRAME_READINGS), jax.random.fold_in(streams_of[1], 1), 0, FRAME_READINGS - 1).astype(jnp.int32),
        "dropout_extent": set_ends(jax.random.randint(streams_of[2], (RECORD_INTERVALS, ROUNDS, UNITS), 0, FRAME_READINGS // 2 + 1), jax.random.fold_in(streams_of[2], 1), 0, (FRAME_READINGS // 2 + 1) - 1).astype(jnp.int32),
        "filter_taps": scatter_about(streams_of[3], (TAPS,), TAPS ** -0.5, 0.5, jnp.float32),
        "source_channel": set_ends(jax.random.randint(streams_of[4], (PAIRS,), 0, ROUNDS), jax.random.fold_in(streams_of[4], 1), 0, ROUNDS - 1).astype(jnp.int32),
        "receiver_block": set_ends(jax.random.randint(streams_of[5], (PAIRS,), 0, 2 * BLOCKS_DEV), jax.random.fold_in(streams_of[5], 1), 0, (2 * BLOCKS_DEV) - 1).astype(jnp.int32),
    }


def valid_mask(starts, lengths, sample_count):
    position = jnp.arange(sample_count, dtype=jnp.int32)
    inside = (position >= starts[..., None]) & (position < starts[..., None] + lengths[..., None])
    return jnp.where(inside, 0.0, 1.0).astype(jnp.float32)

def fir_filter(signal, filter_taps):
    tap_count = filter_taps.shape[0]
    channel_count, sample_count = signal.shape
    pieces = signal.reshape(channel_count, sample_count // tap_count, tap_count)
    earlier = jnp.concatenate([jnp.zeros_like(pieces[:, :1]), pieces[:, :-1]], axis=1)
    position = jnp.arange(tap_count, dtype=jnp.int32)
    offset = position[None, :] - position[:, None]
    present_filter_tap = jnp.where(offset >= 0, filter_taps[jnp.clip(offset, 0, tap_count - 1)], 0.0)
    carried_tap = jnp.where(offset < 0, filter_taps[jnp.clip(offset + tap_count, 0, tap_count - 1)], 0.0)
    result = jnp.einsum('cki,im->ckm', pieces, present_filter_tap, precision=lax.Precision.HIGHEST)
    result = result + jnp.einsum('cki,im->ckm', earlier, carried_tap, precision=lax.Precision.HIGHEST)
    return result.reshape(channel_count, sample_count)

def normalize_traces(filtered, retained_mask):
    counted = lax.optimization_barrier(jnp.sum(retained_mask, axis=-1, keepdims=True))
    mean_square = lax.optimization_barrier(jnp.sum(filtered * filtered * retained_mask, axis=-1, keepdims=True)) / counted
    return (filtered * retained_mask * lax.rsqrt(mean_square + 1e-05)).astype(jnp.bfloat16)

def correlate(source, receivers, max_lag):
    sample_count = source.shape[0]
    padding = jnp.zeros((max_lag,), source.dtype)
    padded = jnp.concatenate([padding, source, padding])
    row_positions = jnp.arange(sample_count, dtype=jnp.int32)[:, None]
    delay_lag_index = jnp.arange(2 * max_lag, dtype=jnp.int32)[None, :]
    toeplitz = padded[row_positions - delay_lag_index + 2 * max_lag]
    return jnp.dot(receivers, toeplitz, preferred_element_type=jnp.float32)

def reference(recordings, gap_start, dropout_extent, filter_taps, source_channel, receiver_block):
    segment_count, round_count, unit_count, sample_count = recordings.shape
    channel_count = round_count * unit_count

    def process_segment(segment_item):
        raw_segment, start_segment, length_segment = segment_item
        traces = raw_segment.reshape(channel_count, sample_count)
        retained_mask = valid_mask(start_segment.reshape(channel_count), length_segment.reshape(channel_count), sample_count)
        filtered = fir_filter(traces * retained_mask, filter_taps)
        return normalize_traces(filtered, retained_mask)
    normalized = lax.map(process_segment, (recordings, gap_start, dropout_extent))
    extended = jnp.concatenate([normalized, jnp.zeros((segment_count, round_count, sample_count), normalized.dtype)], axis=1)
    pair_count = source_channel.shape[0]
    group_index = jnp.arange(pair_count, dtype=jnp.int32) // PAIR_DEV
    source_index = (group_index * round_count + source_channel).astype(jnp.int32)
    receiver_start = (group_index * round_count + receiver_block * BLOCK).astype(jnp.int32)

    def one_pair(pair_item):
        source_at, receiver_at = pair_item
        sources = lax.dynamic_slice_in_dim(extended, source_at, 1, axis=1)[:, 0]
        receivers = lax.dynamic_slice_in_dim(extended, receiver_at, BLOCK, axis=1)

        def add_segment(accumulated_sum, segment_item):
            source_row, listener_rows = segment_item
            return (accumulated_sum + correlate(source_row, listener_rows, MAX_LAG), None)
        accumulated_sum, unused = lax.scan(add_segment, jnp.zeros((BLOCK, 2 * MAX_LAG), jnp.float32), (sources, receivers))
        return accumulated_sum
    stacks = lax.map(one_pair, (source_index, receiver_start))
    factor = 1.0 / math.sqrt(sample_count * segment_count)
    return jnp.transpose(stacks, (1, 0, 2)) * factor
```

```python
import math

import jax
import jax.numpy as jnp
from jax import lax
from jax.experimental import pallas as pl
from jax.experimental.pallas import tpu as pltpu
from jax.sharding import PartitionSpec as P

BLOCK = 128
MAX_LAG = 512
LANES = 128
TILE = 256
NEAR = 4


def toeplitz_rows(row, width):
    return pltpu.roll(
        jnp.broadcast_to(row, (LANES, width)), 0, 1, stride=1, stride_axis=0
    )


def normalize_kernel(
    slots, kept, rec_hbm, start_ref, extent_ref, taps_ref, out_ref, rec_ref, sems
):
    blocks = rec_hbm.shape[0]
    rows = blocks * kept
    pieces = rec_hbm.shape[2] // kept
    sample_count = pieces * LANES
    copies = []
    for slot in range(slots):
        copy = pltpu.make_async_copy(rec_hbm.at[:, slot], rec_ref.at[slot], sems.at[slot])
        copy.start()
        copies.append(copy)
    taps = jnp.concatenate([taps_ref[...], jnp.zeros((1, LANES), jnp.float32)], axis=1)
    weights = toeplitz_rows(taps, 2 * LANES)
    starts = start_ref[...].astype(jnp.float32)
    ends = starts + extent_ref[...].astype(jnp.float32)
    round_count = starts.shape[1]
    lane = lax.broadcasted_iota(jnp.int32, (rows, round_count), 1)
    row = lax.broadcasted_iota(jnp.int32, (rows, round_count), 0)
    position = lax.broadcasted_iota(jnp.int32, (rows, LANES), 1).astype(jnp.float32)
    for slot in range(slots):
        own = lane == (row // kept) * (slots * kept) + slot * kept + row % kept
        start = jnp.sum(jnp.where(own, starts, 0.0), axis=1, keepdims=True)
        end = jnp.sum(jnp.where(own, ends, 0.0), axis=1, keepdims=True)
        counted = sample_count - (jnp.minimum(end, float(sample_count)) - start)
        copies[slot].wait()
        flat = rec_ref.at[slot].reshape(rows * pieces, LANES)
        valids = []
        masked = []
        for piece in range(pieces):
            at = position + float(piece * LANES)
            valid = jnp.where((at >= start) & (at < end), 0.0, 1.0)
            valids.append(valid)
            masked.append(flat[pl.ds(piece, rows, stride=pieces), :] * valid)
        spread = jnp.dot(
            jnp.concatenate(masked, axis=0),
            weights,
            preferred_element_type=jnp.float32,
            precision=lax.Precision.HIGHEST,
        )
        kept_parts = []
        squares = jnp.zeros((rows, LANES), jnp.float32)
        for piece in range(pieces):
            filtered = spread[piece * rows : (piece + 1) * rows, :LANES]
            if piece:
                filtered = filtered + spread[(piece - 1) * rows : piece * rows, LANES:]
            filtered = filtered * valids[piece]
            squares = squares + filtered * filtered
            kept_parts.append(filtered)
        mean_square = jnp.sum(squares, axis=1, keepdims=True) / counted
        scale = lax.rsqrt(mean_square + 1e-05)
        normalized = jnp.concatenate(kept_parts, axis=1) * scale
        out_ref[slot] = normalized.astype(out_ref.dtype)


def normalize(recordings, gap_start, dropout_extent, filter_taps, blocks, slots, kept):
    round_count, sample_count = recordings.shape[1], recordings.shape[3]
    pieces = sample_count // LANES
    view = recordings.reshape(blocks, slots, kept * pieces, LANES)

    def body(*refs):
        normalize_kernel(slots, kept, *refs)

    return pl.pallas_call(
        body,
        out_shape=jax.ShapeDtypeStruct((slots, blocks * kept, sample_count), jnp.bfloat16),
        in_specs=[
            pl.BlockSpec(memory_space=pl.ANY),
            pl.BlockSpec(memory_space=pltpu.VMEM),
            pl.BlockSpec(memory_space=pltpu.VMEM),
            pl.BlockSpec(memory_space=pltpu.VMEM),
        ],
        out_specs=pl.BlockSpec(memory_space=pltpu.VMEM),
        scratch_shapes=[
            pltpu.VMEM((slots, blocks, kept * pieces, LANES), jnp.float32),
            pltpu.SemaphoreType.DMA((slots,)),
        ],
        name="normalize",
    )(
        view,
        gap_start.reshape(1, round_count),
        dropout_extent.reshape(1, round_count),
        filter_taps.reshape(1, LANES),
    )


def pick_kernel(units, kept, segments, channel_ref, got_hbm, out_ref, tiles, sems):
    pair_count = channel_ref.shape[0]
    copies = []
    for pair in range(pair_count):
        unit = channel_ref[pair] % units
        for segment in range(segments):
            at = pair * segments + segment
            copy = pltpu.make_async_copy(
                got_hbm.at[segment * units + unit], tiles.at[at], sems.at[at]
            )
            copy.start()
            copies.append(copy)
    for pair in range(pair_count):
        channel = channel_ref[pair]
        wanted = (channel // BLOCK) * kept + ((channel % BLOCK) // units) % kept
        for segment in range(segments):
            at = pair * segments + segment
            copies[at].wait()
            tile = tiles[at].astype(jnp.float32)
            row = lax.broadcasted_iota(jnp.int32, tile.shape, 0)
            found = jnp.sum(jnp.where(row == wanted, tile, 0.0), axis=0, keepdims=True)
            out_ref[at : at + 1, :] = found


def pick_sources(source_channel, got, units, kept, segments):
    pair_count = source_channel.shape[0]
    chunk_rows, sample_count = got.shape[1:]
    count = pair_count * segments

    def body(*refs):
        pick_kernel(units, kept, segments, *refs)

    return pl.pallas_call(
        body,
        out_shape=jax.ShapeDtypeStruct((count, sample_count), jnp.float32),
        in_specs=[
            pl.BlockSpec(memory_space=pltpu.SMEM),
            pl.BlockSpec(memory_space=pl.ANY),
        ],
        out_specs=pl.BlockSpec(memory_space=pltpu.VMEM),
        scratch_shapes=[
            pltpu.VMEM((count, chunk_rows, sample_count), jnp.bfloat16),
            pltpu.SemaphoreType.DMA((count,)),
        ],
        name="pick_sources",
    )(source_channel, got)


def merge_in_kernel(got_ref, merged_ref, units):
    segments = merged_ref.shape[1]
    upper = lax.broadcasted_iota(jnp.int32, (8, got_ref.shape[2]), 0) < 4
    for segment in range(segments):
        for first in range(0, units, 4):
            parts = [[] for _ in range(NEAR)]
            for unit in (first, first + 2):
                low = got_ref[segment * units + unit].astype(jnp.float32)
                high = got_ref[segment * units + unit + 1].astype(jnp.float32)
                for half in range(2):
                    a = low[8 * half : 8 * half + 8]
                    b = high[8 * half : 8 * half + 8]
                    parts[2 * half].append(jnp.where(upper, a, pltpu.roll(b, 4, 0)))
                    parts[2 * half + 1].append(jnp.where(upper, pltpu.roll(a, 4, 0), b))
            for block in range(NEAR):
                merged_ref[block, segment, first * 4 : first * 4 + 16, :] = jnp.concatenate(
                    parts[block], axis=0
                ).astype(jnp.bfloat16)


def correlate_kernel(
    owned, kept, units, merged_here, channel_ref, block_ref, got_ref, source_ref, out_ref, *scratch
):
    if merged_here:
        merged_ref, lines_ref = scratch
        merge_in_kernel(got_ref, merged_ref, units)
    else:
        merged_ref, (lines_ref,) = got_ref, scratch
    segments, _, sample_count = merged_ref.shape[1:]
    pair_count = channel_ref.shape[0]
    factor = 1.0 / math.sqrt(sample_count * segments)
    halves = sample_count // TILE
    lag_tiles = 2 * MAX_LAG // TILE
    spare = jnp.zeros((1, LANES), jnp.float32)
    edge = jnp.zeros((LANES, LANES), jnp.bfloat16)
    for pair in range(pair_count):
        holder = (channel_ref[pair] % BLOCK) // owned
        block = block_ref[pair]
        sums = [None] * lag_tiles
        for segment in range(segments):
            at = pair * segments + segment
            line = source_ref[holder, at : at + 1, :].astype(jnp.float32)
            moved = toeplitz_rows(
                jnp.concatenate([line, spare], axis=1), sample_count + LANES
            ).astype(jnp.bfloat16)
            padded = jnp.concatenate([edge, moved, edge], axis=1)
            rows = merged_ref[block, segment]
            taken = jnp.concatenate(
                [rows[:, half * TILE : (half + 1) * TILE] for half in range(halves)], axis=0
            )
            for step in range(halves + 1):
                low = step * TILE
                tile = jnp.concatenate(
                    [padded[:, low + LANES : low + LANES + TILE], padded[:, low : low + TILE]],
                    axis=0,
                )
                product = lax.dot_general(
                    taken, tile, (((1,), (1,)), ((), ())), preferred_element_type=jnp.float32
                )
                for half in range(halves):
                    lag_tile = half + MAX_LAG // TILE - step
                    part = product[half * owned : (half + 1) * owned]
                    old = sums[lag_tile]
                    sums[lag_tile] = part if old is None else old + part
        across = owned // kept
        for lag_tile in range(lag_tiles):
            for part in range(TILE // LANES):
                low = part * LANES
                lines_ref[...] = sums[lag_tile][:, low : low + LANES] * factor
                low = low + lag_tile * TILE
                for place in range(kept):
                    out_ref[place * across : (place + 1) * across, pair, low : low + LANES] = (
                        lines_ref[pl.ds(place, across, stride=kept), :]
                    )


def correlate(source_channel, receiver_block, got, sources, owned, kept, units, merged_here):
    pair_count = source_channel.shape[0]
    segments, sample_count = sources.shape[1] // pair_count, sources.shape[2]

    def body(*refs):
        correlate_kernel(owned, kept, units, merged_here, *refs)

    scratch = [pltpu.VMEM((owned, LANES), jnp.float32)]
    if merged_here:
        scratch.insert(0, pltpu.VMEM((NEAR, segments, owned, sample_count), jnp.bfloat16))
    return pl.pallas_call(
        body,
        out_shape=jax.ShapeDtypeStruct((owned, pair_count, 2 * MAX_LAG), jnp.float32),
        in_specs=[
            pl.BlockSpec(memory_space=pltpu.SMEM),
            pl.BlockSpec(memory_space=pltpu.SMEM),
            pl.BlockSpec(memory_space=pltpu.VMEM),
            pl.BlockSpec(memory_space=pltpu.VMEM),
        ],
        out_specs=pl.BlockSpec(memory_space=pltpu.VMEM),
        scratch_shapes=scratch,
        name="correlate",
    )(source_channel, receiver_block, got, sources)


def local(recordings, gap_start, dropout_extent, filter_taps, source_channel, receiver_block):
    round_count, sample_count = recordings.shape[1], recordings.shape[3]
    segments = lax.axis_size("tm")
    units = lax.axis_size("chan")
    groups = units
    blocks = round_count * units // BLOCK
    near = blocks // groups
    owned = BLOCK // segments
    rounds_block = BLOCK // units
    slots = min(segments, rounds_block)
    kept = rounds_block // slots
    normalized = normalize(
        recordings, gap_start, dropout_extent, filter_taps, blocks, slots, kept
    )
    beyond = jnp.zeros((slots, near * kept, sample_count), normalized.dtype)
    extended = jnp.concatenate([normalized, beyond], axis=1)
    windows = jnp.stack(
        [
            extended[:, group * near * kept : (group + 2) * near * kept]
            for group in range(groups)
        ],
        axis=1,
    )
    sent = jnp.repeat(windows, segments // slots, axis=0)
    got = lax.all_to_all(
        sent.reshape(segments * groups, NEAR * kept, sample_count),
        ("tm", "chan"),
        split_axis=0,
        concat_axis=0,
        tiled=True,
    )
    picked = pick_sources(source_channel, got, units, kept, segments)
    sources = lax.all_gather(picked.astype(jnp.bfloat16), "tm")
    merged_here = kept == 4 and owned == 4 * units
    if not merged_here:
        across = owned // kept
        apart = got.reshape(segments, units, NEAR, kept, sample_count)
        first = lax.axis_index("tm") * owned % units
        apart = lax.dynamic_slice_in_dim(apart, first, across, axis=1)
        got = apart.transpose(2, 0, 1, 3, 4).reshape(NEAR, segments, owned, sample_count)
    return correlate(
        source_channel, receiver_block, got, sources, owned, kept, units, merged_here
    )


def solution(mesh):
    return jax.shard_map(
        local,
        mesh=mesh,
        in_specs=(
            P("tm", None, "chan", None),
            P("tm", None, "chan"),
            P("tm", None, "chan"),
            P(),
            P("chan"),
            P("chan"),
        ),
        out_specs=P("tm", "chan", None),
        check_vma=False,
    )
```

```python
import math

import jax
import jax.numpy as jnp
from jax import lax
from jax.experimental import pallas as pl
from jax.experimental.pallas import tpu as pltpu
from jax.sharding import PartitionSpec as P

BLOCK = 128
MAX_LAG = 512
LANES = 128
TILE = 256
NEAR = 4


def toeplitz_rows(row, width):
    return pltpu.roll(
        jnp.broadcast_to(row, (LANES, width)), 0, 1, stride=1, stride_axis=0
    )


def normalize_kernel(
    slots, kept, rec_hbm, start_ref, extent_ref, taps_ref, out_ref, rec_ref, sems
):
    blocks = rec_hbm.shape[0]
    rows = blocks * kept
    pieces = rec_hbm.shape[2] // kept
    sample_count = pieces * LANES
    copies = []
    for slot in range(slots):
        copy = pltpu.make_async_copy(rec_hbm.at[:, slot], rec_ref.at[slot], sems.at[slot])
        copy.start()
        copies.append(copy)
    taps = jnp.concatenate([taps_ref[...], jnp.zeros((1, LANES), jnp.float32)], axis=1)
    weights = toeplitz_rows(taps, 2 * LANES)
    starts = start_ref[...].astype(jnp.float32)
    ends = starts + extent_ref[...].astype(jnp.float32)
    round_count = starts.shape[1]
    lane = lax.broadcasted_iota(jnp.int32, (rows, round_count), 1)
    row = lax.broadcasted_iota(jnp.int32, (rows, round_count), 0)
    position = lax.broadcasted_iota(jnp.int32, (rows, LANES), 1).astype(jnp.float32)
    for slot in range(slots):
        own = lane == (row // kept) * (slots * kept) + slot * kept + row % kept
        start = jnp.sum(jnp.where(own, starts, 0.0), axis=1, keepdims=True)
        end = jnp.sum(jnp.where(own, ends, 0.0), axis=1, keepdims=True)
        counted = sample_count - (jnp.minimum(end, float(sample_count)) - start)
        copies[slot].wait()
        flat = rec_ref.at[slot].reshape(rows * pieces, LANES)
        valids = []
        masked = []
        for piece in range(pieces):
            at = position + float(piece * LANES)
            valid = jnp.where((at >= start) & (at < end), 0.0, 1.0)
            valids.append(valid)
            masked.append(flat[pl.ds(piece, rows, stride=pieces), :] * valid)
        spread = jnp.dot(
            jnp.concatenate(masked, axis=0),
            weights,
            preferred_element_type=jnp.float32,
            precision=lax.Precision.HIGHEST,
        )
        kept_parts = []
        squares = jnp.zeros((rows, LANES), jnp.float32)
        for piece in range(pieces):
            filtered = spread[piece * rows : (piece + 1) * rows, :LANES]
            if piece:
                filtered = filtered + spread[(piece - 1) * rows : piece * rows, LANES:]
            filtered = filtered * valids[piece]
            squares = squares + filtered * filtered
            kept_parts.append(filtered)
        mean_square = jnp.sum(squares, axis=1, keepdims=True) / counted
        scale = lax.rsqrt(mean_square + 1e-05)
        normalized = jnp.concatenate(kept_parts, axis=1) * scale
        out_ref[slot] = normalized.astype(out_ref.dtype)


def normalize(recordings, gap_start, dropout_extent, filter_taps, blocks, slots, kept):
    round_count, sample_count = recordings.shape[1], recordings.shape[3]
    pieces = sample_count // LANES
    view = recordings.reshape(blocks, slots, kept * pieces, LANES)

    def body(*refs):
        normalize_kernel(slots, kept, *refs)

    return pl.pallas_call(
        body,
        out_shape=jax.ShapeDtypeStruct((slots, blocks * kept, sample_count), jnp.bfloat16),
        in_specs=[
            pl.BlockSpec(memory_space=pl.ANY),
            pl.BlockSpec(memory_space=pltpu.VMEM),
            pl.BlockSpec(memory_space=pltpu.VMEM),
            pl.BlockSpec(memory_space=pltpu.VMEM),
        ],
        out_specs=pl.BlockSpec(memory_space=pltpu.VMEM),
        scratch_shapes=[
            pltpu.VMEM((slots, blocks, kept * pieces, LANES), jnp.float32),
            pltpu.SemaphoreType.DMA((slots,)),
        ],
        name="normalize",
    )(
        view,
        gap_start.reshape(1, round_count),
        dropout_extent.reshape(1, round_count),
        filter_taps.reshape(1, LANES),
    )


def pick_kernel(units, kept, segments, channel_ref, got_hbm, out_ref, tiles, sems):
    pair_count = channel_ref.shape[0]
    copies = []
    for pair in range(pair_count):
        unit = channel_ref[pair] % units
        for segment in range(segments):
            at = pair * segments + segment
            copy = pltpu.make_async_copy(
                got_hbm.at[segment * units + unit], tiles.at[at], sems.at[at]
            )
            copy.start()
            copies.append(copy)
    for pair in range(pair_count):
        channel = channel_ref[pair]
        wanted = (channel // BLOCK) * kept + ((channel % BLOCK) // units) % kept
        for segment in range(segments):
            at = pair * segments + segment
            copies[at].wait()
            tile = tiles[at].astype(jnp.float32)
            row = lax.broadcasted_iota(jnp.int32, tile.shape, 0)
            found = jnp.sum(jnp.where(row == wanted, tile, 0.0), axis=0, keepdims=True)
            out_ref[at : at + 1, :] = found.astype(out_ref.dtype)


def pick_sources(source_channel, got, units, kept, segments):
    pair_count = source_channel.shape[0]
    chunk_rows, sample_count = got.shape[1:]
    count = pair_count * segments

    def body(*refs):
        pick_kernel(units, kept, segments, *refs)

    return pl.pallas_call(
        body,
        out_shape=jax.ShapeDtypeStruct((count, sample_count), jnp.bfloat16),
        in_specs=[
            pl.BlockSpec(memory_space=pltpu.SMEM),
            pl.BlockSpec(memory_space=pl.ANY),
        ],
        out_specs=pl.BlockSpec(memory_space=pltpu.VMEM),
        scratch_shapes=[
            pltpu.VMEM((count, chunk_rows, sample_count), jnp.bfloat16),
            pltpu.SemaphoreType.DMA((count,)),
        ],
        name="pick_sources",
    )(source_channel, got)


def merge_in_kernel(got_refs, merged_ref, units):
    segments = merged_ref.shape[1]
    upper = lax.broadcasted_iota(jnp.int32, (8, merged_ref.shape[3]), 0) < 4
    for group, got_ref in enumerate(got_refs):
        for segment in range(segments):
            for first in range(0, units, 4):
                parts = [[], []]
                for unit in (first, first + 2):
                    a = got_ref[segment * units + unit].astype(jnp.float32)
                    b = got_ref[segment * units + unit + 1].astype(jnp.float32)
                    parts[0].append(jnp.where(upper, a, pltpu.roll(b, 4, 0)))
                    parts[1].append(jnp.where(upper, pltpu.roll(a, 4, 0), b))
                for block in range(2):
                    merged_ref[2 * group + block, segment, first * 4 : first * 4 + 16, :] = (
                        jnp.concatenate(parts[block], axis=0).astype(jnp.bfloat16)
                    )


def correlate_kernel(owned, kept, units, merged_here, channel_ref, block_ref, source_ref, *refs):
    if merged_here:
        own_ref, next_ref, out_ref, lines_ref, merged_ref = refs
        merge_in_kernel((own_ref, next_ref), merged_ref, units)
    else:
        merged_ref, out_ref, lines_ref = refs
    segments, _, sample_count = merged_ref.shape[1:]
    pair_count = channel_ref.shape[0]
    factor = 1.0 / math.sqrt(sample_count * segments)
    halves = sample_count // TILE
    lag_tiles = 2 * MAX_LAG // TILE
    spare = jnp.zeros((1, LANES), jnp.float32)
    edge = jnp.zeros((LANES, LANES), jnp.bfloat16)
    for pair in range(pair_count):
        holder = (channel_ref[pair] % BLOCK) // owned
        block = block_ref[pair]
        sums = [None] * lag_tiles
        for segment in range(segments):
            at = pair * segments + segment
            line = source_ref[holder, at : at + 1, :].astype(jnp.float32)
            moved = toeplitz_rows(
                jnp.concatenate([line, spare], axis=1), sample_count + LANES
            ).astype(jnp.bfloat16)
            padded = jnp.concatenate([edge, moved, edge], axis=1)
            rows = merged_ref[block, segment]
            taken = jnp.concatenate(
                [rows[:, half * TILE : (half + 1) * TILE] for half in range(halves)], axis=0
            )
            for step in range(halves + 1):
                low = step * TILE
                tile = jnp.concatenate(
                    [padded[:, low + LANES : low + LANES + TILE], padded[:, low : low + TILE]],
                    axis=0,
                )
                product = lax.dot_general(
                    taken, tile, (((1,), (1,)), ((), ())), preferred_element_type=jnp.float32
                )
                for half in range(halves):
                    lag_tile = half + MAX_LAG // TILE - step
                    part = product[half * owned : (half + 1) * owned]
                    old = sums[lag_tile]
                    sums[lag_tile] = part if old is None else old + part
        across = owned // kept
        for lag_tile in range(lag_tiles):
            for part in range(TILE // LANES):
                low = part * LANES
                lines_ref[...] = sums[lag_tile][:, low : low + LANES] * factor
                low = low + lag_tile * TILE
                for place in range(kept):
                    out_ref[place * across : (place + 1) * across, pair, low : low + LANES] = (
                        lines_ref[pl.ds(place, across, stride=kept), :]
                    )


def correlate(source_channel, receiver_block, sources, receivers, owned, kept, units):
    pair_count = source_channel.shape[0]
    segments, sample_count = sources.shape[1] // pair_count, sources.shape[2]
    merged_here = len(receivers) == 2

    def body(*refs):
        correlate_kernel(owned, kept, units, merged_here, *refs)

    scratch = [pltpu.VMEM((owned, LANES), jnp.float32)]
    if merged_here:
        scratch.append(pltpu.VMEM((NEAR, segments, owned, sample_count), jnp.bfloat16))
    return pl.pallas_call(
        body,
        out_shape=jax.ShapeDtypeStruct((owned, pair_count, 2 * MAX_LAG), jnp.float32),
        in_specs=[pl.BlockSpec(memory_space=pltpu.SMEM)] * 2
        + [pl.BlockSpec(memory_space=pltpu.VMEM)] * (1 + len(receivers)),
        out_specs=pl.BlockSpec(memory_space=pltpu.VMEM),
        scratch_shapes=scratch,
        name="correlate",
    )(source_channel, receiver_block, sources, *receivers)


def local(recordings, gap_start, dropout_extent, filter_taps, source_channel, receiver_block):
    round_count, sample_count = recordings.shape[1], recordings.shape[3]
    segments = lax.axis_size("tm")
    units = lax.axis_size("chan")
    groups = units
    blocks = round_count * units // BLOCK
    near = blocks // groups
    owned = BLOCK // segments
    rounds_block = BLOCK // units
    slots = min(segments, rounds_block)
    kept = rounds_block // slots
    normalized = normalize(
        recordings, gap_start, dropout_extent, filter_taps, blocks, slots, kept
    )
    sent = normalized.reshape(slots, groups, near * kept, sample_count)
    sent = jnp.repeat(sent, segments // slots, axis=0) if segments > slots else sent
    got = lax.all_to_all(
        sent.reshape(segments * groups, near * kept, sample_count),
        ("tm", "chan"),
        split_axis=0,
        concat_axis=0,
        tiled=True,
    )
    following = lax.ppermute(got, "chan", [(group, group - 1) for group in range(1, groups)])
    picked = pick_sources(source_channel, got, units, kept, segments)
    sources = lax.all_gather(picked, "tm")
    receivers = (got, following)
    if kept != 4 or owned != 4 * units or near != 2:
        across = owned // kept
        first = lax.axis_index("tm") * owned % units
        apart = [x.reshape(segments, units, near, kept, sample_count) for x in receivers]
        apart = lax.dynamic_slice_in_dim(jnp.concatenate(apart, axis=2), first, across, axis=1)
        receivers = (
            apart.transpose(2, 0, 1, 3, 4).reshape(2 * near, segments, owned, sample_count),
        )
    return correlate(source_channel, receiver_block, sources, receivers, owned, kept, units)


def solution(mesh):
    return jax.shard_map(
        local,
        mesh=mesh,
        in_specs=(
            P("tm", None, "chan", None),
            P("tm", None, "chan"),
            P("tm", None, "chan"),
            P(),
            P("chan"),
            P("chan"),
        ),
        out_specs=P("tm", "chan", None),
        check_vma=False,
    )
```

```python
import math

import jax
import jax.numpy as jnp
from jax import lax
from jax.experimental import pallas as pl
from jax.experimental.pallas import tpu as pltpu
from jax.sharding import PartitionSpec as P

BLOCK = 128
MAX_LAG = 512
LANES = 128
TILE = 256
NEAR = 4


def near_core(x):
    return pltpu.with_memory_space_constraint(x, pltpu.VMEM)


def toeplitz_rows(row, width, first=0):
    return pltpu.roll(
        jnp.broadcast_to(row, (LANES, width)), first, 1, stride=1, stride_axis=0
    )


def normalize_kernel(
    slots, kept, rec_hbm, start_ref, extent_ref, taps_ref, out_ref, rec_ref, sems
):
    blocks = rec_hbm.shape[0]
    rows = blocks * kept
    pieces = rec_hbm.shape[2] // kept
    sample_count = pieces * LANES
    copies = []
    for slot in range(slots):
        copy = pltpu.make_async_copy(rec_hbm.at[:, slot], rec_ref.at[slot], sems.at[slot])
        copy.start()
        copies.append(copy)
    taps = jnp.concatenate([taps_ref[...], jnp.zeros((1, LANES), jnp.float32)], axis=1)
    weights = toeplitz_rows(taps, 2 * LANES)
    starts = start_ref[...].astype(jnp.float32)
    ends = starts + extent_ref[...].astype(jnp.float32)
    round_count = starts.shape[1]
    lane = lax.broadcasted_iota(jnp.int32, (rows, round_count), 1)
    row = lax.broadcasted_iota(jnp.int32, (rows, round_count), 0)
    position = lax.broadcasted_iota(jnp.int32, (rows, LANES), 1).astype(jnp.float32)
    spans = []
    for slot in range(slots):
        own = lane == (row // kept) * (slots * kept) + slot * kept + row % kept
        start = jnp.sum(jnp.where(own, starts, 0.0), axis=1, keepdims=True)
        end = jnp.sum(jnp.where(own, ends, 0.0), axis=1, keepdims=True)
        spans.append((start, end, sample_count - (jnp.minimum(end, float(sample_count)) - start)))
    for copy in copies:
        copy.wait()
    for slot in range(slots):
        start, end, counted = spans[slot]
        flat = rec_ref.at[slot].reshape(rows * pieces, LANES)
        valids = []
        masked = []
        for piece in range(pieces):
            at = position + float(piece * LANES)
            valid = jnp.where((at >= start) & (at < end), 0.0, 1.0)
            valids.append(valid)
            masked.append(flat[pl.ds(piece, rows, stride=pieces), :] * valid)
        spread = jnp.dot(
            jnp.concatenate(masked, axis=0),
            weights,
            preferred_element_type=jnp.float32,
            precision=lax.Precision.HIGHEST,
        )
        kept_parts = []
        squares = jnp.zeros((rows, LANES), jnp.float32)
        for piece in range(pieces):
            filtered = spread[piece * rows : (piece + 1) * rows, :LANES]
            if piece:
                filtered = filtered + spread[(piece - 1) * rows : piece * rows, LANES:]
            filtered = filtered * valids[piece]
            squares = squares + filtered * filtered
            kept_parts.append(filtered)
        mean_square = jnp.sum(squares, axis=1, keepdims=True) / counted
        scale = lax.rsqrt(mean_square + 1e-05)
        normalized = jnp.concatenate(kept_parts, axis=1) * scale
        out_ref[slot] = normalized.astype(out_ref.dtype)


def normalize(recordings, gap_start, dropout_extent, filter_taps, blocks, slots, kept):
    round_count, sample_count = recordings.shape[1], recordings.shape[3]
    pieces = sample_count // LANES
    view = recordings.reshape(blocks, slots, kept * pieces, LANES)

    def body(*refs):
        normalize_kernel(slots, kept, *refs)

    return pl.pallas_call(
        body,
        out_shape=pltpu.VMEM((slots, blocks * kept, sample_count), jnp.bfloat16),
        in_specs=[
            pl.BlockSpec(memory_space=pl.ANY),
            pl.BlockSpec(memory_space=pltpu.VMEM),
            pl.BlockSpec(memory_space=pltpu.VMEM),
            pl.BlockSpec(memory_space=pltpu.VMEM),
        ],
        out_specs=pl.BlockSpec(memory_space=pltpu.VMEM),
        scratch_shapes=[
            pltpu.VMEM((slots, blocks, kept * pieces, LANES), jnp.float32),
            pltpu.SemaphoreType.DMA((slots,)),
        ],
        name="normalize",
    )(
        view,
        gap_start.reshape(1, round_count),
        dropout_extent.reshape(1, round_count),
        filter_taps.reshape(1, LANES),
    )


def pick_kernel(units, kept, segments, channel_ref, got_ref, out_ref):
    sample_count = got_ref.shape[2]
    shape = got_ref.shape[1:]
    row = lax.broadcasted_iota(jnp.int32, shape, 0)
    found = []
    for pair in range(channel_ref.shape[0]):
        channel = channel_ref[pair]
        unit = channel % units
        wanted = row == (channel // BLOCK) * kept + ((channel % BLOCK) // units) % kept
        for segment in range(segments):
            tile = got_ref[segment * units + unit].astype(jnp.float32)
            found.append(jnp.sum(jnp.where(wanted, tile, 0.0), axis=0, keepdims=True))
    lines = jnp.concatenate(found, axis=0).astype(jnp.bfloat16)
    swap = lax.broadcasted_iota(jnp.int32, (LANES, LANES), 0) + lax.broadcasted_iota(
        jnp.int32, (LANES, LANES), 1
    )
    swap = jnp.where(swap == LANES - 1, 1.0, 0.0).astype(jnp.bfloat16)
    for low in range(0, sample_count, LANES):
        high = sample_count - low
        out_ref[:, low : low + LANES] = jnp.dot(
            lines[:, high - LANES : high], swap, preferred_element_type=jnp.float32
        ).astype(out_ref.dtype)


def pick_sources(source_channel, got, units, kept, segments):
    count = source_channel.shape[0] * segments

    def body(*refs):
        pick_kernel(units, kept, segments, *refs)

    return pl.pallas_call(
        body,
        out_shape=pltpu.VMEM((count, got.shape[2]), jnp.bfloat16),
        in_specs=[
            pl.BlockSpec(memory_space=pltpu.SMEM),
            pl.BlockSpec(memory_space=pltpu.VMEM),
        ],
        out_specs=pl.BlockSpec(memory_space=pltpu.VMEM),
        name="pick_sources",
    )(source_channel, near_core(got))


def merge_in_kernel(got_refs, merged_ref, units):
    segments = merged_ref.shape[1]
    upper = lax.broadcasted_iota(jnp.int32, (8, merged_ref.shape[3]), 0) < 4
    for group, got_ref in enumerate(got_refs):
        for segment in range(segments):
            for first in range(0, units, 4):
                parts = [[], []]
                for unit in (first, first + 2):
                    a = got_ref[segment * units + unit].astype(jnp.float32)
                    b = got_ref[segment * units + unit + 1].astype(jnp.float32)
                    parts[0].append(jnp.where(upper, a, pltpu.roll(b, 4, 0)))
                    parts[1].append(jnp.where(upper, pltpu.roll(a, 4, 0), b))
                for block in range(2):
                    merged_ref[2 * group + block, segment, first * 4 : first * 4 + 16, :] = (
                        jnp.concatenate(parts[block], axis=0).astype(jnp.bfloat16)
                    )


def correlate_kernel(owned, kept, units, merged_here, channel_ref, block_ref, source_ref, *refs):
    if merged_here:
        own_ref, next_ref, out_ref, lines_ref, merged_ref = refs
        merge_in_kernel((own_ref, next_ref), merged_ref, units)
    else:
        merged_ref, out_ref, lines_ref = refs
    segments, _, sample_count = merged_ref.shape[1:]
    pair_count = channel_ref.shape[0]
    factor = 1.0 / math.sqrt(sample_count * segments)
    halves = sample_count // TILE
    lag_tiles = 2 * MAX_LAG // TILE
    spare = jnp.zeros((1, LANES), jnp.float32)
    edge = jnp.zeros((LANES, LANES), jnp.bfloat16)
    for pair in range(pair_count):
        holder = (channel_ref[pair] % BLOCK) // owned
        block = block_ref[pair]
        sums = [None] * lag_tiles
        for segment in range(segments):
            at = pair * segments + segment
            line = source_ref[holder, at : at + 1, :].astype(jnp.float32)
            moved = toeplitz_rows(
                jnp.concatenate([line, spare], axis=1), sample_count + LANES, 1
            ).astype(jnp.bfloat16)
            padded = jnp.concatenate([edge, moved, edge], axis=1)
            rows = merged_ref[block, segment]
            taken = jnp.concatenate(
                [rows[:, half * TILE : (half + 1) * TILE] for half in range(halves)], axis=0
            )
            for step in range(halves + 1):
                low = sample_count - step * TILE
                tile = jnp.concatenate(
                    [padded[:, low + LANES : low + LANES + TILE], padded[:, low : low + TILE]],
                    axis=0,
                )
                product = jnp.dot(taken, tile, preferred_element_type=jnp.float32)
                for half in range(halves):
                    lag_tile = half + MAX_LAG // TILE - step
                    part = product[half * owned : (half + 1) * owned]
                    old = sums[lag_tile]
                    sums[lag_tile] = part if old is None else old + part
        across = owned // kept
        for lag_tile in range(lag_tiles):
            for part in range(TILE // LANES):
                low = part * LANES
                lines_ref[...] = sums[lag_tile][:, low : low + LANES] * factor
                low = low + lag_tile * TILE
                for place in range(kept):
                    out_ref[place * across : (place + 1) * across, pair, low : low + LANES] = (
                        lines_ref[pl.ds(place, across, stride=kept), :]
                    )


def correlate(source_channel, receiver_block, sources, receivers, owned, kept, units):
    pair_count = source_channel.shape[0]
    segments, sample_count = sources.shape[1] // pair_count, sources.shape[2]
    merged_here = len(receivers) == 2

    def body(*refs):
        correlate_kernel(owned, kept, units, merged_here, *refs)

    scratch = [pltpu.VMEM((owned, LANES), jnp.float32)]
    if merged_here:
        scratch.append(pltpu.VMEM((NEAR, segments, owned, sample_count), jnp.bfloat16))
    return pl.pallas_call(
        body,
        out_shape=jax.ShapeDtypeStruct((owned, pair_count, 2 * MAX_LAG), jnp.float32),
        in_specs=[pl.BlockSpec(memory_space=pltpu.SMEM)] * 2
        + [pl.BlockSpec(memory_space=pltpu.VMEM)] * (1 + len(receivers)),
        out_specs=pl.BlockSpec(memory_space=pltpu.VMEM),
        scratch_shapes=scratch,
        name="correlate",
    )(source_channel, receiver_block, near_core(sources), *map(near_core, receivers))


def local(recordings, gap_start, dropout_extent, filter_taps, source_channel, receiver_block):
    round_count, sample_count = recordings.shape[1], recordings.shape[3]
    segments = lax.axis_size("tm")
    units = lax.axis_size("chan")
    groups = units
    blocks = round_count * units // BLOCK
    near = blocks // groups
    owned = BLOCK // segments
    rounds_block = BLOCK // units
    slots = min(segments, rounds_block)
    kept = rounds_block // slots
    normalized = normalize(
        recordings, gap_start, dropout_extent, filter_taps, blocks, slots, kept
    )
    sent = normalized.reshape(slots, groups, near * kept, sample_count)
    sent = jnp.repeat(sent, segments // slots, axis=0) if segments > slots else sent
    got = lax.all_to_all(
        sent.reshape(segments * groups, near * kept, sample_count),
        ("tm", "chan"),
        split_axis=0,
        concat_axis=0,
        tiled=True,
    )
    following = lax.ppermute(got, "chan", [(group, group - 1) for group in range(1, groups)])
    picked = pick_sources(source_channel, got, units, kept, segments)
    sources = lax.all_gather(picked, "tm")
    receivers = (got, following)
    if kept != 4 or owned != 4 * units or near != 2:
        across = owned // kept
        first = lax.axis_index("tm") * owned % units
        apart = [x.reshape(segments, units, near, kept, sample_count) for x in receivers]
        apart = lax.dynamic_slice_in_dim(jnp.concatenate(apart, axis=2), first, across, axis=1)
        receivers = (
            apart.transpose(2, 0, 1, 3, 4).reshape(2 * near, segments, owned, sample_count),
        )
    return correlate(source_channel, receiver_block, sources, receivers, owned, kept, units)


def solution(mesh):
    return jax.shard_map(
        local,
        mesh=mesh,
        in_specs=(
            P("tm", None, "chan", None),
            P("tm", None, "chan"),
            P("tm", None, "chan"),
            P(),
            P("chan"),
            P("chan"),
        ),
        out_specs=P("tm", "chan", None),
        check_vma=False,
    )
```

```python
import math

import jax
import jax.numpy as jnp
from jax import lax
from jax.experimental import pallas as pl
from jax.experimental.pallas import tpu as pltpu
from jax.sharding import PartitionSpec as P

BLOCK = 128
MAX_LAG = 512
LANES = 128
KERNEL_VMEM = 24 << 20
NEAR = 4


def near_core(x):
    return pltpu.with_memory_space_constraint(x, pltpu.VMEM)


def far(x):
    return pltpu.with_memory_space_constraint(x, pltpu.HBM)


def toeplitz_rows(row, width, first=0):
    return pltpu.roll(
        jnp.broadcast_to(row, (LANES, width)), first, 1, stride=1, stride_axis=0
    )


def normalize_kernel(
    slots, kept, rec_hbm, start_ref, extent_ref, taps_ref, out_ref, rec_ref, sems
):
    blocks = rec_hbm.shape[0]
    rows = blocks * kept
    pieces = rec_hbm.shape[2] // kept
    sample_count = pieces * LANES
    copies = []
    for slot in range(slots):
        copy = pltpu.make_async_copy(rec_hbm.at[:, slot], rec_ref.at[slot], sems.at[slot])
        copy.start()
        copies.append(copy)
    taps = jnp.concatenate([taps_ref[...], jnp.zeros((1, LANES), jnp.float32)], axis=1)
    weights = toeplitz_rows(taps, 2 * LANES)
    starts = start_ref[...].astype(jnp.float32)
    ends = starts + extent_ref[...].astype(jnp.float32)
    round_count = starts.shape[1]
    lane = lax.broadcasted_iota(jnp.int32, (rows, round_count), 1)
    row = lax.broadcasted_iota(jnp.int32, (rows, round_count), 0)
    position = lax.broadcasted_iota(jnp.int32, (rows, LANES), 1).astype(jnp.float32)
    spans = []
    for slot in range(slots):
        own = lane == (row // kept) * (slots * kept) + slot * kept + row % kept
        start = jnp.sum(jnp.where(own, starts, 0.0), axis=1, keepdims=True)
        end = jnp.sum(jnp.where(own, ends, 0.0), axis=1, keepdims=True)
        spans.append((start, end, sample_count - (jnp.minimum(end, float(sample_count)) - start)))
    for copy in copies:
        copy.wait()
    for slot in range(slots):
        start, end, counted = spans[slot]
        flat = rec_ref.at[slot].reshape(rows * pieces, LANES)
        valids = []
        masked = []
        for piece in range(pieces):
            at = position + float(piece * LANES)
            valid = jnp.where((at >= start) & (at < end), 0.0, 1.0)
            valids.append(valid)
            masked.append(flat[pl.ds(piece, rows, stride=pieces), :] * valid)
        spread = jnp.dot(
            jnp.concatenate(masked, axis=0),
            weights,
            preferred_element_type=jnp.float32,
            precision=lax.Precision.HIGHEST,
        )
        kept_parts = []
        squares = jnp.zeros((rows, LANES), jnp.float32)
        for piece in range(pieces):
            filtered = spread[piece * rows : (piece + 1) * rows, :LANES]
            if piece:
                filtered = filtered + spread[(piece - 1) * rows : piece * rows, LANES:]
            filtered = filtered * valids[piece]
            squares = squares + filtered * filtered
            kept_parts.append(filtered)
        mean_square = jnp.sum(squares, axis=1, keepdims=True) / counted
        scale = lax.rsqrt(mean_square + 1e-05)
        normalized = jnp.concatenate(kept_parts, axis=1) * scale
        out_ref[slot] = normalized.astype(out_ref.dtype)


def normalize(recordings, gap_start, dropout_extent, filter_taps, blocks, slots, kept):
    round_count, sample_count = recordings.shape[1], recordings.shape[3]
    pieces = sample_count // LANES
    view = recordings.reshape(blocks, slots, kept * pieces, LANES)

    def body(*refs):
        normalize_kernel(slots, kept, *refs)

    return pl.pallas_call(
        body,
        out_shape=pltpu.VMEM((slots, blocks * kept, sample_count), jnp.bfloat16),
        in_specs=[
            pl.BlockSpec(memory_space=pl.ANY),
            pl.BlockSpec(memory_space=pltpu.VMEM),
            pl.BlockSpec(memory_space=pltpu.VMEM),
            pl.BlockSpec(memory_space=pltpu.VMEM),
        ],
        out_specs=pl.BlockSpec(memory_space=pltpu.VMEM),
        scratch_shapes=[
            pltpu.VMEM((slots, blocks, kept * pieces, LANES), jnp.float32),
            pltpu.SemaphoreType.DMA((slots,)),
        ],
        name="normalize",
    )(
        view,
        gap_start.reshape(1, round_count),
        dropout_extent.reshape(1, round_count),
        filter_taps.reshape(1, LANES),
    )


def pick_kernel(units, kept, segments, channel_ref, got_ref, out_ref):
    sample_count = got_ref.shape[2]
    shape = got_ref.shape[1:]
    row = lax.broadcasted_iota(jnp.int32, shape, 0)
    found = []
    for pair in range(channel_ref.shape[0]):
        channel = channel_ref[pair]
        unit = channel % units
        wanted = row == (channel // BLOCK) * kept + ((channel % BLOCK) // units) % kept
        for segment in range(segments):
            tile = got_ref[segment * units + unit].astype(jnp.float32)
            found.append(jnp.sum(jnp.where(wanted, tile, 0.0), axis=0, keepdims=True))
    lines = jnp.concatenate(found, axis=0).astype(jnp.bfloat16)
    swap = lax.broadcasted_iota(jnp.int32, (LANES, LANES), 0) + lax.broadcasted_iota(
        jnp.int32, (LANES, LANES), 1
    )
    swap = jnp.where(swap == LANES - 1, 1.0, 0.0).astype(jnp.bfloat16)
    for low in range(0, sample_count, LANES):
        high = sample_count - low
        out_ref[:, low : low + LANES] = jnp.dot(
            lines[:, high - LANES : high], swap, preferred_element_type=jnp.float32
        ).astype(out_ref.dtype)


def pick_sources(source_channel, got, units, kept, segments):
    count = source_channel.shape[0] * segments

    def body(*refs):
        pick_kernel(units, kept, segments, *refs)

    return pl.pallas_call(
        body,
        out_shape=pltpu.VMEM((count, got.shape[2]), jnp.bfloat16),
        in_specs=[
            pl.BlockSpec(memory_space=pltpu.SMEM),
            pl.BlockSpec(memory_space=pltpu.VMEM),
        ],
        out_specs=pl.BlockSpec(memory_space=pltpu.VMEM),
        name="pick_sources",
    )(far(source_channel), near_core(got))


def merge_in_kernel(got_ref, merged_ref, units):
    upper = lax.broadcasted_iota(jnp.int32, (8, merged_ref.shape[3]), 0) < 4
    for segment in range(merged_ref.shape[1]):
        for first in range(0, units, 4):
            parts = [[], []]
            for unit in (first, first + 2):
                a = got_ref[segment * units + unit].astype(jnp.float32)
                b = got_ref[segment * units + unit + 1].astype(jnp.float32)
                parts[0].append(jnp.where(upper, a, pltpu.roll(b, 4, 0)))
                parts[1].append(jnp.where(upper, pltpu.roll(a, 4, 0), b))
            for block in range(2):
                merged_ref[block, segment, first * 4 : first * 4 + 16, :] = jnp.concatenate(
                    parts[block], axis=0
                ).astype(jnp.bfloat16)


def prepare_kernel(owned, units, merged_here, channel_ref, source_ref, *refs):
    if merged_here:
        own_ref, moved_ref, merged_ref = refs
        merge_in_kernel(own_ref, merged_ref, units)
    else:
        (moved_ref,) = refs
    pair_count = channel_ref.shape[0]
    segments = source_ref.shape[1] // pair_count
    spare = jnp.zeros((1, LANES), jnp.float32)
    for pair in range(pair_count):
        holder = (channel_ref[pair] % BLOCK) // owned
        for segment in range(segments):
            at = pair * segments + segment
            line = source_ref[holder, at : at + 1, :].astype(jnp.float32)
            line = jnp.concatenate([line, spare], axis=1)
            moved_ref[at] = toeplitz_rows(line, line.shape[1], 1).astype(jnp.bfloat16)


def prepare(source_channel, sources, own, owned, units):
    pair_count = source_channel.shape[0]
    count, sample_count = sources.shape[1:]
    out_shape = [pltpu.VMEM((count, LANES, sample_count + LANES), jnp.bfloat16)]
    if own:
        merged = (NEAR // 2, count // pair_count, owned, sample_count)
        out_shape.append(pltpu.VMEM(merged, jnp.bfloat16))

    def body(*refs):
        prepare_kernel(owned, units, bool(own), *refs)

    return pl.pallas_call(
        body,
        out_shape=out_shape,
        in_specs=[pl.BlockSpec(memory_space=pltpu.SMEM)]
        + [pl.BlockSpec(memory_space=pltpu.VMEM)] * (1 + len(own)),
        out_specs=[pl.BlockSpec(memory_space=pltpu.VMEM)] * len(out_shape),
        compiler_params=pltpu.CompilerParams(vmem_limit_bytes=KERNEL_VMEM),
        name="prepare",
    )(far(source_channel), near_core(sources), *map(near_core, own))


def lag_products(receivers, toeplitz):
    rows, sample_count = receivers[0].shape
    pieces = sample_count // LANES
    empty = jnp.zeros((rows, LANES), receivers[0].dtype)
    sides = []
    stacked = []
    pairs = []
    last = []
    for row, moved in zip(receivers, toeplitz, strict=True):
        parts = [row[:, i * LANES : (i + 1) * LANES] for i in range(pieces)]
        tiles = [
            moved[:, (pieces - i) * LANES : (pieces - i + 1) * LANES] for i in range(pieces + 1)
        ]
        sides.append(jnp.concatenate([empty, *parts], axis=0))
        sides.append(jnp.concatenate([*parts, empty], axis=0))
        stacked.append(jnp.concatenate(parts, axis=0))
        pairs.append(jnp.concatenate(tiles[0:pieces:2], axis=1))
        pairs.append(jnp.concatenate(tiles[1:pieces:2], axis=1))
        last.append(tiles[pieces])
    first = jnp.dot(
        jnp.concatenate(sides, axis=1),
        jnp.concatenate(pairs, axis=0),
        preferred_element_type=jnp.float32,
    )
    second = jnp.dot(
        jnp.concatenate(stacked, axis=1),
        jnp.concatenate(last, axis=0),
        preferred_element_type=jnp.float32,
    )
    sums = [None] * (2 * pieces)
    for i in range(pieces):
        sums[i] = second[i * rows : (i + 1) * rows]
    for column in range(pieces // 2):
        for i in range(pieces + 1):
            part = first[i * rows : (i + 1) * rows, column * LANES : (column + 1) * LANES]
            chunk = i - 1 + pieces - 2 * column
            sums[chunk] = part if sums[chunk] is None else sums[chunk] + part
    return sums


def correlate_kernel(owned, kept, units, merged_here, block_ref, moved_ref, *refs):
    if merged_here:
        own_ref, next_ref, out_hbm, lines_ref, out_ref, sems, after_ref = refs
        merge_in_kernel(next_ref, after_ref, units)
        segments, _, sample_count = own_ref.shape[1:]
    else:
        merged_ref, out_hbm, lines_ref, out_ref, sems = refs
        segments, _, sample_count = merged_ref.shape[1:]
    pair_count = block_ref.shape[0]
    factor = 1.0 / math.sqrt(sample_count * segments)
    across = owned // kept
    copies = []
    for pair in range(pair_count):
        block = block_ref[pair]
        if merged_here:
            ahead = block >= NEAR // 2
            place = block % (NEAR // 2)
            receivers = [
                jnp.where(ahead, after_ref[place, i], own_ref[place, i]) for i in range(segments)
            ]
        else:
            receivers = [merged_ref[block, i] for i in range(segments)]
        sums = lag_products(receivers, [moved_ref[pair * segments + i] for i in range(segments)])
        for chunk, part in enumerate(sums):
            lines_ref[chunk] = part * factor
            low = chunk * LANES
            for place in range(kept):
                out_ref[place * across : (place + 1) * across, pair, low : low + LANES] = (
                    lines_ref[chunk, pl.ds(place, across, stride=kept), :]
                )
        copy = pltpu.make_async_copy(out_ref.at[:, pair], out_hbm.at[:, pair], sems.at[pair])
        copy.start()
        copies.append(copy)
    for copy in copies:
        copy.wait()


def correlate(receiver_block, toeplitz, receivers, owned, kept, units):
    pair_count = receiver_block.shape[0]
    merged_here = len(receivers) == 2
    shape = (owned, pair_count, 2 * MAX_LAG)

    def body(*refs):
        correlate_kernel(owned, kept, units, merged_here, *refs)

    scratch = [
        pltpu.VMEM((2 * MAX_LAG // LANES, owned, LANES), jnp.float32),
        pltpu.VMEM(shape, jnp.float32),
        pltpu.SemaphoreType.DMA((pair_count,)),
    ]
    if merged_here:
        scratch.append(pltpu.VMEM(receivers[0].shape, jnp.bfloat16))
    return pl.pallas_call(
        body,
        out_shape=jax.ShapeDtypeStruct(shape, jnp.float32),
        in_specs=[pl.BlockSpec(memory_space=pltpu.SMEM)]
        + [pl.BlockSpec(memory_space=pltpu.VMEM)] * (1 + len(receivers)),
        out_specs=pl.BlockSpec(memory_space=pl.ANY),
        scratch_shapes=scratch,
        compiler_params=pltpu.CompilerParams(vmem_limit_bytes=KERNEL_VMEM),
        name="correlate",
    )(far(receiver_block), near_core(toeplitz), *map(near_core, receivers))


def local(recordings, gap_start, dropout_extent, filter_taps, source_channel, receiver_block):
    round_count, sample_count = recordings.shape[1], recordings.shape[3]
    segments = lax.axis_size("tm")
    units = lax.axis_size("chan")
    groups = units
    blocks = round_count * units // BLOCK
    near = blocks // groups
    owned = BLOCK // segments
    rounds_block = BLOCK // units
    slots = min(segments, rounds_block)
    kept = rounds_block // slots
    normalized = normalize(
        recordings, gap_start, dropout_extent, filter_taps, blocks, slots, kept
    )
    sent = normalized.reshape(slots, groups, near * kept, sample_count)
    sent = jnp.repeat(sent, segments // slots, axis=0) if segments > slots else sent
    got = lax.all_to_all(
        sent.reshape(segments * groups, near * kept, sample_count),
        ("tm", "chan"),
        split_axis=0,
        concat_axis=0,
        tiled=True,
    )
    following = lax.ppermute(got, "chan", [(group, group - 1) for group in range(1, groups)])
    picked = pick_sources(source_channel, got, units, kept, segments)
    sources = lax.all_gather(picked, "tm")
    if kept == 4 and owned == 4 * units and near == 2:
        toeplitz, own = prepare(source_channel, sources, (got,), owned, units)
        return correlate(receiver_block, toeplitz, (own, following), owned, kept, units)
    across = owned // kept
    first = lax.axis_index("tm") * owned % units
    apart = [x.reshape(segments, units, near, kept, sample_count) for x in (got, following)]
    apart = lax.dynamic_slice_in_dim(jnp.concatenate(apart, axis=2), first, across, axis=1)
    merged = apart.transpose(2, 0, 1, 3, 4).reshape(2 * near, segments, owned, sample_count)
    (toeplitz,) = prepare(source_channel, sources, (), owned, units)
    return correlate(receiver_block, toeplitz, (merged,), owned, kept, units)


def solution(mesh):
    return jax.shard_map(
        local,
        mesh=mesh,
        in_specs=(
            P("tm", None, "chan", None),
            P("tm", None, "chan"),
            P("tm", None, "chan"),
            P(),
            P("chan"),
            P("chan"),
        ),
        out_specs=P("tm", "chan", None),
        check_vma=False,
    )
```

```python
import math

import jax
import jax.numpy as jnp
from jax import lax
from jax.experimental import pallas as pl
from jax.experimental.pallas import tpu as pltpu
from jax.sharding import PartitionSpec as P

BLOCK = 128
MAX_LAG = 512
PAIR_DEV = 4
LANES = 128
KERNEL_VMEM = 24 << 20
NEAR = 4


def near_core(x):
    return pltpu.with_memory_space_constraint(x, pltpu.VMEM)


def toeplitz_rows(row, width, first=0):
    return pltpu.roll(
        jnp.broadcast_to(row, (LANES, width)), first, 1, stride=1, stride_axis=0
    )


def in_parts(x):
    first = x.astype(jnp.bfloat16)
    rest = x - first.astype(jnp.float32)
    second = rest.astype(jnp.bfloat16)
    return first, second, (rest - second.astype(jnp.float32)).astype(jnp.bfloat16)


def normalize_kernel(slots, kept, rec_hbm, *refs):
    small_refs, (out_ref, index_ref, rec_ref), small_bufs, sems = (
        refs[:5],
        refs[5:8],
        refs[8:13],
        refs[13],
    )
    blocks = rec_hbm.shape[0]
    rows = blocks * kept
    pieces = rec_hbm.shape[2] // kept
    sample_count = pieces * LANES
    small = []
    for i, (small_ref, small_buf) in enumerate(zip(small_refs, small_bufs, strict=True)):
        copy = pltpu.make_async_copy(small_ref, small_buf, sems.at[slots + i])
        copy.start()
        small.append(copy)
    copies = []
    for slot in range(slots):
        copy = pltpu.make_async_copy(rec_hbm.at[:, slot], rec_ref.at[slot], sems.at[slot])
        copy.start()
        copies.append(copy)
    for copy in small:
        copy.wait()
    taps_ref, start_ref, extent_ref, channel_ref, block_ref = small_bufs
    taps = jnp.concatenate([taps_ref[...], jnp.zeros((1, LANES), jnp.float32)], axis=1)
    w0, w1, w2 = in_parts(toeplitz_rows(taps, 2 * LANES))
    weights = jnp.concatenate([w0, w0, w0, w1, w1, w2], axis=0)
    starts = start_ref[...].astype(jnp.float32)
    ends = starts + extent_ref[...].astype(jnp.float32)
    for i, ref in enumerate((channel_ref, block_ref)):
        for pair in range(PAIR_DEV):
            value = jnp.broadcast_to(ref[:, pair : pair + 1], (1, LANES))
            index_ref[i * PAIR_DEV + pair : i * PAIR_DEV + pair + 1, :] = value
    round_count = starts.shape[1]
    lane = lax.broadcasted_iota(jnp.int32, (rows, round_count), 1)
    row = lax.broadcasted_iota(jnp.int32, (rows, round_count), 0)
    position = lax.broadcasted_iota(jnp.int32, (rows, LANES), 1).astype(jnp.float32)
    spans = []
    for slot in range(slots):
        own = lane == (row // kept) * (slots * kept) + slot * kept + row % kept
        start = jnp.sum(jnp.where(own, starts, 0.0), axis=1, keepdims=True)
        end = jnp.sum(jnp.where(own, ends, 0.0), axis=1, keepdims=True)
        spans.append((start, end, sample_count - (jnp.minimum(end, float(sample_count)) - start)))
    for copy in copies:
        copy.wait()
    for slot in range(slots):
        start, end, counted = spans[slot]
        flat = rec_ref.at[slot].reshape(rows * pieces, LANES)
        valids = []
        masked = []
        for piece in range(pieces):
            at = position + float(piece * LANES)
            valid = jnp.where((at >= start) & (at < end), 0.0, 1.0)
            valids.append(valid)
            masked.append(flat[pl.ds(piece, rows, stride=pieces), :] * valid)
        x0, x1, x2 = in_parts(jnp.concatenate(masked, axis=0))
        spread = jnp.dot(
            jnp.concatenate([x0, x1, x2, x0, x1, x0], axis=1),
            weights,
            preferred_element_type=jnp.float32,
        )
        kept_parts = []
        squares = jnp.zeros((rows, LANES), jnp.float32)
        for piece in range(pieces):
            filtered = spread[piece * rows : (piece + 1) * rows, :LANES]
            if piece:
                filtered = filtered + spread[(piece - 1) * rows : piece * rows, LANES:]
            filtered = filtered * valids[piece]
            squares = squares + filtered * filtered
            kept_parts.append(filtered)
        mean_square = jnp.sum(squares, axis=1, keepdims=True) / counted
        scale = lax.rsqrt(mean_square + 1e-05)
        normalized = jnp.concatenate(kept_parts, axis=1) * scale
        out_ref[slot] = normalized.astype(out_ref.dtype)


def normalize(recordings, small, blocks, slots, kept):
    sample_count = recordings.shape[3]
    pieces = sample_count // LANES
    view = recordings.reshape(blocks, slots, kept * pieces, LANES)

    def body(*refs):
        normalize_kernel(slots, kept, *refs)

    return pl.pallas_call(
        body,
        out_shape=(
            pltpu.VMEM((slots, blocks * kept, sample_count), jnp.bfloat16),
            pltpu.VMEM((2 * PAIR_DEV, LANES), jnp.int32),
        ),
        in_specs=[pl.BlockSpec(memory_space=pl.ANY)] * (1 + len(small)),
        out_specs=[pl.BlockSpec(memory_space=pltpu.VMEM)] * 2,
        scratch_shapes=[
            pltpu.VMEM((slots, blocks, kept * pieces, LANES), jnp.float32),
            *[pltpu.VMEM(x.shape, x.dtype) for x in small],
            pltpu.SemaphoreType.DMA((slots + len(small),)),
        ],
        name="normalize",
    )(view, *small)


def index_at(index_ref, row):
    return jnp.max(index_ref[row : row + 1, :].astype(jnp.float32)).astype(jnp.int32)


def pick_kernel(units, kept, segments, index_ref, got_ref, out_ref):
    sample_count = got_ref.shape[2]
    shape = got_ref.shape[1:]
    row = lax.broadcasted_iota(jnp.int32, shape, 0)
    found = []
    for pair in range(PAIR_DEV):
        channel = index_at(index_ref, pair)
        unit = channel % units
        wanted = row == (channel // BLOCK) * kept + ((channel % BLOCK) // units) % kept
        for segment in range(segments):
            tile = got_ref[segment * units + unit].astype(jnp.float32)
            found.append(jnp.sum(jnp.where(wanted, tile, 0.0), axis=0, keepdims=True))
    lines = jnp.concatenate(found, axis=0).astype(jnp.bfloat16)
    swap = lax.broadcasted_iota(jnp.int32, (LANES, LANES), 0) + lax.broadcasted_iota(
        jnp.int32, (LANES, LANES), 1
    )
    swap = jnp.where(swap == LANES - 1, 1.0, 0.0).astype(jnp.bfloat16)
    for low in range(0, sample_count, LANES):
        high = sample_count - low
        out_ref[:, low : low + LANES] = jnp.dot(
            lines[:, high - LANES : high], swap, preferred_element_type=jnp.float32
        ).astype(out_ref.dtype)


def pick_sources(index, got, units, kept, segments):
    count = PAIR_DEV * segments

    def body(*refs):
        pick_kernel(units, kept, segments, *refs)

    return pl.pallas_call(
        body,
        out_shape=pltpu.VMEM((count, got.shape[2]), jnp.bfloat16),
        in_specs=[
            pl.BlockSpec(memory_space=pltpu.VMEM),
            pl.BlockSpec(memory_space=pltpu.VMEM),
        ],
        out_specs=pl.BlockSpec(memory_space=pltpu.VMEM),
        name="pick_sources",
    )(near_core(index), near_core(got))


def merge_in_kernel(got_ref, merged_ref, units):
    upper = lax.broadcasted_iota(jnp.int32, (8, merged_ref.shape[3]), 0) < 4
    for segment in range(merged_ref.shape[1]):
        for first in range(0, units, 4):
            parts = [[], []]
            for unit in (first, first + 2):
                a = got_ref[segment * units + unit].astype(jnp.float32)
                b = got_ref[segment * units + unit + 1].astype(jnp.float32)
                parts[0].append(jnp.where(upper, a, pltpu.roll(b, 4, 0)))
                parts[1].append(jnp.where(upper, pltpu.roll(a, 4, 0), b))
            for block in range(2):
                merged_ref[block, segment, first * 4 : first * 4 + 16, :] = jnp.concatenate(
                    parts[block], axis=0
                ).astype(jnp.bfloat16)


def prepare_kernel(owned, units, merged_here, index_ref, source_ref, *refs):
    if merged_here:
        own_ref, moved_ref, merged_ref = refs
        merge_in_kernel(own_ref, merged_ref, units)
    else:
        (moved_ref,) = refs
    segments = source_ref.shape[1] // PAIR_DEV
    spare = jnp.zeros((1, LANES), jnp.float32)
    for pair in range(PAIR_DEV):
        holder = (index_at(index_ref, pair) % BLOCK) // owned
        for segment in range(segments):
            at = pair * segments + segment
            line = source_ref[holder, at : at + 1, :].astype(jnp.float32)
            line = jnp.concatenate([line, spare], axis=1)
            moved_ref[at] = toeplitz_rows(line, line.shape[1], 1).astype(jnp.bfloat16)


def prepare(index, sources, own, owned, units):
    count, sample_count = sources.shape[1:]
    out_shape = [pltpu.VMEM((count, LANES, sample_count + LANES), jnp.bfloat16)]
    if own:
        merged = (NEAR // 2, count // PAIR_DEV, owned, sample_count)
        out_shape.append(pltpu.VMEM(merged, jnp.bfloat16))

    def body(*refs):
        prepare_kernel(owned, units, bool(own), *refs)

    return pl.pallas_call(
        body,
        out_shape=out_shape,
        in_specs=[pl.BlockSpec(memory_space=pltpu.VMEM)] * (2 + len(own)),
        out_specs=[pl.BlockSpec(memory_space=pltpu.VMEM)] * len(out_shape),
        compiler_params=pltpu.CompilerParams(vmem_limit_bytes=KERNEL_VMEM),
        name="prepare",
    )(near_core(index), near_core(sources), *map(near_core, own))


def lag_products(receivers, toeplitz):
    rows, sample_count = receivers[0].shape
    pieces = sample_count // LANES
    empty = jnp.zeros((rows, LANES), receivers[0].dtype)
    sides = []
    stacked = []
    pairs = []
    last = []
    for row, moved in zip(receivers, toeplitz, strict=True):
        parts = [row[:, i * LANES : (i + 1) * LANES] for i in range(pieces)]
        tiles = [
            moved[:, (pieces - i) * LANES : (pieces - i + 1) * LANES] for i in range(pieces + 1)
        ]
        sides.append(jnp.concatenate([empty, *parts], axis=0))
        sides.append(jnp.concatenate([*parts, empty], axis=0))
        stacked.append(jnp.concatenate(parts, axis=0))
        pairs.append(jnp.concatenate(tiles[0:pieces:2], axis=1))
        pairs.append(jnp.concatenate(tiles[1:pieces:2], axis=1))
        last.append(tiles[pieces])
    first = jnp.dot(
        jnp.concatenate(sides, axis=1),
        jnp.concatenate(pairs, axis=0),
        preferred_element_type=jnp.float32,
    )
    second = jnp.dot(
        jnp.concatenate(stacked, axis=1),
        jnp.concatenate(last, axis=0),
        preferred_element_type=jnp.float32,
    )
    sums = [None] * (2 * pieces)
    for i in range(pieces):
        sums[i] = second[i * rows : (i + 1) * rows]
    for column in range(pieces // 2):
        for i in range(pieces + 1):
            part = first[i * rows : (i + 1) * rows, column * LANES : (column + 1) * LANES]
            chunk = i - 1 + pieces - 2 * column
            sums[chunk] = part if sums[chunk] is None else sums[chunk] + part
    return sums


def correlate_kernel(owned, kept, units, merged_here, index_ref, moved_ref, *refs):
    if merged_here:
        own_ref, next_ref, out_hbm, lines_ref, out_ref, sems, after_ref = refs
        merge_in_kernel(next_ref, after_ref, units)
        segments, _, sample_count = own_ref.shape[1:]
    else:
        merged_ref, out_hbm, lines_ref, out_ref, sems = refs
        segments, _, sample_count = merged_ref.shape[1:]
    factor = 1.0 / math.sqrt(sample_count * segments)
    across = owned // kept
    copies = []
    for pair in range(PAIR_DEV):
        block = index_at(index_ref, PAIR_DEV + pair)
        if merged_here:
            ahead = block >= NEAR // 2
            place = block % (NEAR // 2)
            receivers = [
                jnp.where(ahead, after_ref[place, i], own_ref[place, i]) for i in range(segments)
            ]
        else:
            receivers = [merged_ref[block, i] for i in range(segments)]
        sums = lag_products(receivers, [moved_ref[pair * segments + i] for i in range(segments)])
        for chunk, part in enumerate(sums):
            lines_ref[chunk] = part * factor
            low = chunk * LANES
            for place in range(kept):
                out_ref[place * across : (place + 1) * across, pair, low : low + LANES] = (
                    lines_ref[chunk, pl.ds(place, across, stride=kept), :]
                )
        copy = pltpu.make_async_copy(out_ref.at[:, pair], out_hbm.at[:, pair], sems.at[pair])
        copy.start()
        copies.append(copy)
    for copy in copies:
        copy.wait()


def correlate(index, toeplitz, receivers, owned, kept, units):
    merged_here = len(receivers) == 2
    shape = (owned, PAIR_DEV, 2 * MAX_LAG)

    def body(*refs):
        correlate_kernel(owned, kept, units, merged_here, *refs)

    scratch = [
        pltpu.VMEM((2 * MAX_LAG // LANES, owned, LANES), jnp.float32),
        pltpu.VMEM(shape, jnp.float32),
        pltpu.SemaphoreType.DMA((PAIR_DEV,)),
    ]
    if merged_here:
        scratch.append(pltpu.VMEM(receivers[0].shape, jnp.bfloat16))
    return pl.pallas_call(
        body,
        out_shape=jax.ShapeDtypeStruct(shape, jnp.float32),
        in_specs=[pl.BlockSpec(memory_space=pltpu.VMEM)] * (2 + len(receivers)),
        out_specs=pl.BlockSpec(memory_space=pl.ANY),
        scratch_shapes=scratch,
        compiler_params=pltpu.CompilerParams(vmem_limit_bytes=KERNEL_VMEM),
        name="correlate",
    )(near_core(index), near_core(toeplitz), *map(near_core, receivers))


def local(recordings, gap_start, dropout_extent, filter_taps, source_channel, receiver_block):
    round_count, sample_count = recordings.shape[1], recordings.shape[3]
    segments = lax.axis_size("tm")
    units = lax.axis_size("chan")
    groups = units
    blocks = round_count * units // BLOCK
    near = blocks // groups
    owned = BLOCK // segments
    rounds_block = BLOCK // units
    slots = min(segments, rounds_block)
    kept = rounds_block // slots
    small = [
        x.reshape(1, x.size)
        for x in (filter_taps, gap_start, dropout_extent, source_channel, receiver_block)
    ]
    normalized, index = normalize(recordings, small, blocks, slots, kept)
    sent = normalized.reshape(slots, groups, near * kept, sample_count)
    sent = jnp.repeat(sent, segments // slots, axis=0) if segments > slots else sent
    got = lax.all_to_all(
        sent.reshape(segments * groups, near * kept, sample_count),
        ("tm", "chan"),
        split_axis=0,
        concat_axis=0,
        tiled=True,
    )
    following = lax.ppermute(got, "chan", [(group, group - 1) for group in range(1, groups)])
    picked = pick_sources(index, got, units, kept, segments)
    sources = lax.all_gather(picked, "tm")
    if kept == 4 and owned == 4 * units and near == 2:
        toeplitz, own = prepare(index, sources, (got,), owned, units)
        return correlate(index, toeplitz, (own, following), owned, kept, units)
    across = owned // kept
    first = lax.axis_index("tm") * owned % units
    apart = [x.reshape(segments, units, near, kept, sample_count) for x in (got, following)]
    apart = lax.dynamic_slice_in_dim(jnp.concatenate(apart, axis=2), first, across, axis=1)
    merged = apart.transpose(2, 0, 1, 3, 4).reshape(2 * near, segments, owned, sample_count)
    (toeplitz,) = prepare(index, sources, (), owned, units)
    return correlate(index, toeplitz, (merged,), owned, kept, units)


def solution(mesh):
    return jax.shard_map(
        local,
        mesh=mesh,
        in_specs=(
            P("tm", None, "chan", None),
            P("tm", None, "chan"),
            P("tm", None, "chan"),
            P(),
            P("chan"),
            P("chan"),
        ),
        out_specs=P("tm", "chan", None),
        check_vma=False,
    )
```

```python
import math

import jax
import jax.numpy as jnp
from jax import lax
from jax.experimental import pallas as pl
from jax.experimental.pallas import tpu as pltpu
from jax.sharding import PartitionSpec as P

BLOCK = 128
MAX_LAG = 512
PAIR_DEV = 4
LANES = 128
KERNEL_VMEM = 24 << 20
NEAR = 4


def near_core(x):
    return pltpu.with_memory_space_constraint(x, pltpu.VMEM)


def toeplitz_rows(row, width, first=0):
    return pltpu.roll(
        jnp.broadcast_to(row, (LANES, width)), first, 1, stride=1, stride_axis=0
    )


def in_parts(x):
    first = x.astype(jnp.bfloat16)
    rest = x - first.astype(jnp.float32)
    second = rest.astype(jnp.bfloat16)
    return first, second, (rest - second.astype(jnp.float32)).astype(jnp.bfloat16)


def normalize_kernel(slots, kept, rec_hbm, *refs):
    small_refs, (out_ref, index_ref, rec_ref), small_bufs, sems = (
        refs[:5],
        refs[5:8],
        refs[8:13],
        refs[13],
    )
    blocks = rec_hbm.shape[0]
    rows = blocks * kept
    pieces = rec_hbm.shape[2] // kept
    sample_count = pieces * LANES
    small = []
    for i, (small_ref, small_buf) in enumerate(zip(small_refs, small_bufs, strict=True)):
        copy = pltpu.make_async_copy(small_ref, small_buf, sems.at[slots + i])
        copy.start()
        small.append(copy)
    copies = []
    for slot in range(slots):
        copy = pltpu.make_async_copy(rec_hbm.at[:, slot], rec_ref.at[slot], sems.at[slot])
        copy.start()
        copies.append(copy)
    for copy in small:
        copy.wait()
    taps_ref, start_ref, extent_ref, channel_ref, block_ref = small_bufs
    taps = jnp.concatenate([taps_ref[...], jnp.zeros((1, LANES), jnp.float32)], axis=1)
    w0, w1, w2 = in_parts(toeplitz_rows(taps, 2 * LANES))
    weights = jnp.concatenate([w0, w0, w0, w1, w1, w2], axis=0)
    starts = start_ref[...].astype(jnp.float32)
    ends = starts + extent_ref[...].astype(jnp.float32)
    for i, ref in enumerate((channel_ref, block_ref)):
        for pair in range(PAIR_DEV):
            value = jnp.broadcast_to(ref[:, pair : pair + 1], (1, LANES))
            index_ref[i * PAIR_DEV + pair : i * PAIR_DEV + pair + 1, :] = value
    round_count = starts.shape[1]
    lane = lax.broadcasted_iota(jnp.int32, (rows, round_count), 1)
    row = lax.broadcasted_iota(jnp.int32, (rows, round_count), 0)
    position = lax.broadcasted_iota(jnp.int32, (rows, LANES), 1).astype(jnp.float32)
    spans = []
    for slot in range(slots):
        own = lane == (row // kept) * (slots * kept) + slot * kept + row % kept
        start = jnp.sum(jnp.where(own, starts, 0.0), axis=1, keepdims=True)
        end = jnp.sum(jnp.where(own, ends, 0.0), axis=1, keepdims=True)
        spans.append((start, end, sample_count - (jnp.minimum(end, float(sample_count)) - start)))
    for copy in copies:
        copy.wait()
    for slot in range(slots):
        start, end, counted = spans[slot]
        flat = rec_ref.at[slot].reshape(rows * pieces, LANES)
        valids = []
        masked = []
        for piece in range(pieces):
            at = position + float(piece * LANES)
            valid = jnp.where((at >= start) & (at < end), 0.0, 1.0)
            valids.append(valid)
            masked.append(flat[pl.ds(piece, rows, stride=pieces), :] * valid)
        x0, x1, x2 = in_parts(jnp.concatenate(masked, axis=0))
        spread = jnp.dot(
            jnp.concatenate([x0, x1, x2, x0, x1, x0], axis=1),
            weights,
            preferred_element_type=jnp.float32,
        )
        kept_parts = []
        squares = jnp.zeros((rows, LANES), jnp.float32)
        for piece in range(pieces):
            filtered = spread[piece * rows : (piece + 1) * rows, :LANES]
            if piece:
                filtered = filtered + spread[(piece - 1) * rows : piece * rows, LANES:]
            filtered = filtered * valids[piece]
            squares = squares + filtered * filtered
            kept_parts.append(filtered)
        mean_square = jnp.sum(squares, axis=1, keepdims=True) / counted
        scale = lax.rsqrt(mean_square + 1e-05)
        normalized = jnp.concatenate(kept_parts, axis=1) * scale
        out_ref[slot] = normalized.astype(out_ref.dtype)


def normalize(recordings, small, blocks, slots, kept):
    sample_count = recordings.shape[3]
    pieces = sample_count // LANES
    view = recordings.reshape(blocks, slots, kept * pieces, LANES)

    def body(*refs):
        normalize_kernel(slots, kept, *refs)

    return pl.pallas_call(
        body,
        out_shape=(
            pltpu.VMEM((slots, blocks * kept, sample_count), jnp.bfloat16),
            pltpu.VMEM((2 * PAIR_DEV, LANES), jnp.int32),
        ),
        in_specs=[pl.BlockSpec(memory_space=pl.ANY)] * (1 + len(small)),
        out_specs=[pl.BlockSpec(memory_space=pltpu.VMEM)] * 2,
        scratch_shapes=[
            pltpu.VMEM((slots, blocks, kept * pieces, LANES), jnp.float32),
            *[pltpu.VMEM(x.shape, x.dtype) for x in small],
            pltpu.SemaphoreType.DMA((slots + len(small),)),
        ],
        name="normalize",
    )(view, *small)


def index_at(index_ref, row):
    return jnp.max(index_ref[row : row + 1, :].astype(jnp.float32)).astype(jnp.int32)


def pick_kernel(units, kept, segments, index_ref, got_ref, out_ref):
    sample_count = got_ref.shape[2]
    shape = got_ref.shape[1:]
    row = lax.broadcasted_iota(jnp.int32, shape, 0)
    found = []
    for pair in range(PAIR_DEV):
        channel = index_at(index_ref, pair)
        unit = channel % units
        wanted = row == (channel // BLOCK) * kept + ((channel % BLOCK) // units) % kept
        for segment in range(segments):
            tile = got_ref[segment * units + unit].astype(jnp.float32)
            found.append(jnp.sum(jnp.where(wanted, tile, 0.0), axis=0, keepdims=True))
    lines = jnp.concatenate(found, axis=0).astype(jnp.bfloat16)
    swap = lax.broadcasted_iota(jnp.int32, (LANES, LANES), 0) + lax.broadcasted_iota(
        jnp.int32, (LANES, LANES), 1
    )
    swap = jnp.where(swap == LANES - 1, 1.0, 0.0).astype(jnp.bfloat16)
    for low in range(0, sample_count, LANES):
        high = sample_count - low
        out_ref[:, low : low + LANES] = jnp.dot(
            lines[:, high - LANES : high], swap, preferred_element_type=jnp.float32
        ).astype(out_ref.dtype)


def pick_sources(index, got, units, kept, segments):
    count = PAIR_DEV * segments

    def body(*refs):
        pick_kernel(units, kept, segments, *refs)

    return pl.pallas_call(
        body,
        out_shape=pltpu.VMEM((count, got.shape[2]), jnp.bfloat16),
        in_specs=[
            pl.BlockSpec(memory_space=pltpu.VMEM),
            pl.BlockSpec(memory_space=pltpu.VMEM),
        ],
        out_specs=pl.BlockSpec(memory_space=pltpu.VMEM),
        name="pick_sources",
    )(near_core(index), near_core(got))


def merge_in_kernel(got_ref, merged_ref, spread_ref, units):
    sample_count = merged_ref.shape[3]
    for segment in range(merged_ref.shape[1]):
        for chunk in range(sample_count // LANES):
            low = chunk * LANES
            tile = got_ref[segment * units : (segment + 1) * units, :, low : low + LANES]
            spread_ref[segment, chunk] = tile.astype(jnp.float32).reshape(units * 8, LANES)
            for block in range(2):
                rows = [
                    spread_ref[segment, chunk, pl.ds(block * 4 + place, units, stride=8), :]
                    for place in range(4)
                ]
                merged_ref[block, segment, :, low : low + LANES] = jnp.concatenate(
                    rows, axis=0
                ).astype(jnp.bfloat16)


def spread_like(segments, sample_count, units):
    return pltpu.VMEM((segments, sample_count // LANES, units * 8, LANES), jnp.float32)


def prepare_kernel(owned, units, merged_here, index_ref, source_ref, *refs):
    if merged_here:
        own_ref, moved_ref, merged_ref, spread_ref = refs
        merge_in_kernel(own_ref, merged_ref, spread_ref, units)
    else:
        (moved_ref,) = refs
    segments = source_ref.shape[1] // PAIR_DEV
    spare = jnp.zeros((1, LANES), jnp.float32)
    for pair in range(PAIR_DEV):
        holder = (index_at(index_ref, pair) % BLOCK) // owned
        for segment in range(segments):
            at = pair * segments + segment
            line = source_ref[holder, at : at + 1, :].astype(jnp.float32)
            line = jnp.concatenate([line, spare], axis=1)
            moved_ref[at] = toeplitz_rows(line, line.shape[1], 1).astype(jnp.bfloat16)


def prepare(index, sources, own, owned, units):
    count, sample_count = sources.shape[1:]
    segments = count // PAIR_DEV
    out_shape = [pltpu.VMEM((count, LANES, sample_count + LANES), jnp.bfloat16)]
    scratch = []
    if own:
        merged = (NEAR // 2, segments, owned, sample_count)
        out_shape.append(pltpu.VMEM(merged, jnp.bfloat16))
        scratch.append(spread_like(segments, sample_count, units))

    def body(*refs):
        prepare_kernel(owned, units, bool(own), *refs)

    return pl.pallas_call(
        body,
        out_shape=out_shape,
        in_specs=[pl.BlockSpec(memory_space=pltpu.VMEM)] * (2 + len(own)),
        out_specs=[pl.BlockSpec(memory_space=pltpu.VMEM)] * len(out_shape),
        scratch_shapes=scratch,
        compiler_params=pltpu.CompilerParams(vmem_limit_bytes=KERNEL_VMEM),
        name="prepare",
    )(near_core(index), near_core(sources), *map(near_core, own))


def lag_products(receivers, toeplitz):
    rows, sample_count = receivers[0].shape
    pieces = sample_count // LANES
    empty = jnp.zeros((rows, LANES), receivers[0].dtype)
    sides = []
    stacked = []
    pairs = []
    last = []
    for row, moved in zip(receivers, toeplitz, strict=True):
        parts = [row[:, i * LANES : (i + 1) * LANES] for i in range(pieces)]
        tiles = [
            moved[:, (pieces - i) * LANES : (pieces - i + 1) * LANES] for i in range(pieces + 1)
        ]
        sides.append(jnp.concatenate([empty, *parts], axis=0))
        sides.append(jnp.concatenate([*parts, empty], axis=0))
        stacked.append(jnp.concatenate(parts, axis=0))
        pairs.append(jnp.concatenate(tiles[0:pieces:2], axis=1))
        pairs.append(jnp.concatenate(tiles[1:pieces:2], axis=1))
        last.append(tiles[pieces])
    first = jnp.dot(
        jnp.concatenate(sides, axis=1),
        jnp.concatenate(pairs, axis=0),
        preferred_element_type=jnp.float32,
    )
    second = jnp.dot(
        jnp.concatenate(stacked, axis=1),
        jnp.concatenate(last, axis=0),
        preferred_element_type=jnp.float32,
    )
    sums = [None] * (2 * pieces)
    for i in range(pieces):
        sums[i] = second[i * rows : (i + 1) * rows]
    for column in range(pieces // 2):
        for i in range(pieces + 1):
            part = first[i * rows : (i + 1) * rows, column * LANES : (column + 1) * LANES]
            chunk = i - 1 + pieces - 2 * column
            sums[chunk] = part if sums[chunk] is None else sums[chunk] + part
    return sums


def correlate_kernel(units, merged_here, index_ref, moved_ref, *refs):
    if merged_here:
        own_ref, next_ref, out_hbm, out_ref, sems, after_ref, spread_ref = refs
        segments, _, sample_count = own_ref.shape[1:]
    else:
        merged_ref, out_hbm, out_ref, sems = refs
        segments, _, sample_count = merged_ref.shape[1:]
    factor = 1.0 / math.sqrt(sample_count * segments)
    picked = [index_at(index_ref, PAIR_DEV + pair) for pair in range(PAIR_DEV)]
    if merged_here:
        merge_in_kernel(next_ref, after_ref, spread_ref, units)
    copies = []
    for pair, block in enumerate(picked):
        if merged_here:
            ahead = block >= NEAR // 2
            place = block % (NEAR // 2)
            receivers = [
                jnp.where(ahead, after_ref[place, i], own_ref[place, i]) for i in range(segments)
            ]
        else:
            receivers = [merged_ref[block, i] for i in range(segments)]
        sums = lag_products(receivers, [moved_ref[pair * segments + i] for i in range(segments)])
        for chunk, part in enumerate(sums):
            out_ref[:, pair, chunk * LANES : (chunk + 1) * LANES] = part * factor
        copy = pltpu.make_async_copy(out_ref.at[:, pair], out_hbm.at[:, pair], sems.at[pair])
        copy.start()
        copies.append(copy)
    for copy in copies:
        copy.wait()


def correlate(index, toeplitz, receivers, owned, units):
    merged_here = len(receivers) == 2
    shape = (owned, PAIR_DEV, 2 * MAX_LAG)

    def body(*refs):
        correlate_kernel(units, merged_here, *refs)

    scratch = [
        pltpu.VMEM(shape, jnp.float32),
        pltpu.SemaphoreType.DMA((PAIR_DEV,)),
    ]
    if merged_here:
        own = receivers[0]
        scratch.append(pltpu.VMEM(own.shape, own.dtype))
        scratch.append(spread_like(own.shape[1], own.shape[3], units))
    return pl.pallas_call(
        body,
        out_shape=jax.ShapeDtypeStruct(shape, jnp.float32),
        in_specs=[pl.BlockSpec(memory_space=pltpu.VMEM)] * (2 + len(receivers)),
        out_specs=pl.BlockSpec(memory_space=pl.ANY),
        scratch_shapes=scratch,
        compiler_params=pltpu.CompilerParams(vmem_limit_bytes=KERNEL_VMEM),
        name="correlate",
    )(near_core(index), near_core(toeplitz), *map(near_core, receivers))


def local(recordings, gap_start, dropout_extent, filter_taps, source_channel, receiver_block):
    round_count, sample_count = recordings.shape[1], recordings.shape[3]
    segments = lax.axis_size("tm")
    units = lax.axis_size("chan")
    groups = units
    blocks = round_count * units // BLOCK
    near = blocks // groups
    owned = BLOCK // segments
    rounds_block = BLOCK // units
    slots = min(segments, rounds_block)
    kept = rounds_block // slots
    small = [
        x.reshape(1, x.size)
        for x in (filter_taps, gap_start, dropout_extent, source_channel, receiver_block)
    ]
    normalized, index = normalize(recordings, small, blocks, slots, kept)
    sent = normalized.reshape(slots, groups, near * kept, sample_count)
    sent = jnp.repeat(sent, segments // slots, axis=0) if segments > slots else sent
    got = lax.all_to_all(
        sent.reshape(segments * groups, near * kept, sample_count),
        ("tm", "chan"),
        split_axis=0,
        concat_axis=0,
        tiled=True,
    )
    following = lax.ppermute(got, "chan", [(group, group - 1) for group in range(1, groups)])
    picked = pick_sources(index, got, units, kept, segments)
    sources = lax.all_gather(picked, "tm")
    if kept == 4 and owned == 4 * units and near == 2:
        toeplitz, own = prepare(index, sources, (got,), owned, units)
        return correlate(index, toeplitz, (own, following), owned, units)
    across = owned // kept
    first = lax.axis_index("tm") * owned % units
    apart = [x.reshape(segments, units, near, kept, sample_count) for x in (got, following)]
    apart = lax.dynamic_slice_in_dim(jnp.concatenate(apart, axis=2), first, across, axis=1)
    merged = apart.transpose(2, 0, 3, 1, 4).reshape(2 * near, segments, owned, sample_count)
    (toeplitz,) = prepare(index, sources, (), owned, units)
    return correlate(index, toeplitz, (merged,), owned, units)


def solution(mesh):
    return jax.shard_map(
        local,
        mesh=mesh,
        in_specs=(
            P("tm", None, "chan", None),
            P("tm", None, "chan"),
            P("tm", None, "chan"),
            P(),
            P("chan"),
            P("chan"),
        ),
        out_specs=P("tm", "chan", None),
        check_vma=False,
    )
```

```python
import math

import jax
import jax.numpy as jnp
from jax import lax
from jax.experimental import pallas as pl
from jax.experimental.pallas import tpu as pltpu
from jax.sharding import PartitionSpec as P

BLOCK = 128
MAX_LAG = 512
PAIR_DEV = 4
LANES = 128
KERNEL_VMEM = 24 << 20
NEAR = 4


def near_core(x):
    return pltpu.with_memory_space_constraint(x, pltpu.VMEM)


def in_scalar(x):
    return pltpu.with_memory_space_constraint(x, pltpu.SMEM)


def toeplitz_rows(row, width, first=0):
    return pltpu.roll(
        jnp.broadcast_to(row, (LANES, width)), first, 1, stride=1, stride_axis=0
    )


def in_parts(x):
    first = x.astype(jnp.bfloat16)
    rest = x - first.astype(jnp.float32)
    second = rest.astype(jnp.bfloat16)
    return first, second, (rest - second.astype(jnp.float32)).astype(jnp.bfloat16)


def normalize_kernel(slots, kept, rec_hbm, *refs):
    small_refs, out_ref = refs[:5], refs[5]
    rec_ref, taps_ref, start_ref, extent_ref, sems = refs[8:]
    small_bufs = (taps_ref, start_ref, extent_ref, refs[6], refs[7])
    blocks = rec_hbm.shape[0]
    rows = blocks * kept
    pieces = rec_hbm.shape[2] // kept
    sample_count = pieces * LANES
    small = []
    for i, (small_ref, small_buf) in enumerate(zip(small_refs, small_bufs, strict=True)):
        copy = pltpu.make_async_copy(small_ref, small_buf, sems.at[slots + i])
        copy.start()
        small.append(copy)
    copies = []
    for slot in range(slots):
        copy = pltpu.make_async_copy(rec_hbm.at[:, slot], rec_ref.at[slot], sems.at[slot])
        copy.start()
        copies.append(copy)
    for copy in small:
        copy.wait()
    taps = jnp.concatenate([taps_ref[...], jnp.zeros((1, LANES), jnp.float32)], axis=1)
    w0, w1, w2 = in_parts(toeplitz_rows(taps, 2 * LANES))
    weights = jnp.concatenate([w0, w0, w0, w1, w1, w2], axis=0)
    starts = start_ref[...].astype(jnp.float32)
    ends = starts + extent_ref[...].astype(jnp.float32)
    round_count = starts.shape[1]
    lane = lax.broadcasted_iota(jnp.int32, (rows, round_count), 1)
    row = lax.broadcasted_iota(jnp.int32, (rows, round_count), 0)
    position = lax.broadcasted_iota(jnp.int32, (rows, LANES), 1).astype(jnp.float32)
    spans = []
    for slot in range(slots):
        own = lane == (row // kept) * (slots * kept) + slot * kept + row % kept
        start = jnp.sum(jnp.where(own, starts, 0.0), axis=1, keepdims=True)
        end = jnp.sum(jnp.where(own, ends, 0.0), axis=1, keepdims=True)
        spans.append((start, end, sample_count - (jnp.minimum(end, float(sample_count)) - start)))
    for copy in copies:
        copy.wait()
    for slot in range(slots):
        start, end, counted = spans[slot]
        flat = rec_ref.at[slot].reshape(rows * pieces, LANES)
        valids = []
        masked = []
        for piece in range(pieces):
            at = position + float(piece * LANES)
            valid = jnp.where((at >= start) & (at < end), 0.0, 1.0)
            valids.append(valid)
            masked.append(flat[pl.ds(piece, rows, stride=pieces), :] * valid)
        x0, x1, x2 = in_parts(jnp.concatenate(masked, axis=0))
        spread = jnp.dot(
            jnp.concatenate([x0, x1, x2, x0, x1, x0], axis=1),
            weights,
            preferred_element_type=jnp.float32,
        )
        kept_parts = []
        squares = jnp.zeros((rows, LANES), jnp.float32)
        for piece in range(pieces):
            filtered = spread[piece * rows : (piece + 1) * rows, :LANES]
            if piece:
                filtered = filtered + spread[(piece - 1) * rows : piece * rows, LANES:]
            filtered = filtered * valids[piece]
            squares = squares + filtered * filtered
            kept_parts.append(filtered)
        mean_square = jnp.sum(squares, axis=1, keepdims=True) / counted
        scale = lax.rsqrt(mean_square + 1e-05)
        normalized = jnp.concatenate(kept_parts, axis=1) * scale
        out_ref[slot] = normalized.astype(out_ref.dtype)


def normalize(recordings, small, blocks, slots, kept):
    sample_count = recordings.shape[3]
    pieces = sample_count // LANES
    view = recordings.reshape(blocks, slots, kept * pieces, LANES)

    def body(*refs):
        normalize_kernel(slots, kept, *refs)

    return pl.pallas_call(
        body,
        out_shape=(
            pltpu.VMEM((slots, blocks * kept, sample_count), jnp.bfloat16),
            pltpu.SMEM((PAIR_DEV,), jnp.int32),
            pltpu.SMEM((PAIR_DEV,), jnp.int32),
        ),
        in_specs=[pl.BlockSpec(memory_space=pl.ANY)] * (1 + len(small)),
        out_specs=[pl.BlockSpec(memory_space=pltpu.VMEM)]
        + [pl.BlockSpec(memory_space=pltpu.SMEM)] * 2,
        scratch_shapes=[
            pltpu.VMEM((slots, blocks, kept * pieces, LANES), jnp.float32),
            *[pltpu.VMEM(x.shape, x.dtype) for x in small[:3]],
            pltpu.SemaphoreType.DMA((slots + len(small),)),
        ],
        name="normalize",
    )(view, *small)


def pick_kernel(units, kept, segments, channel_ref, got_ref, out_ref):
    sample_count = got_ref.shape[2]
    shape = got_ref.shape[1:]
    row = lax.broadcasted_iota(jnp.int32, shape, 0)
    found = []
    for pair in range(PAIR_DEV):
        channel = channel_ref[pair]
        unit = channel % units
        wanted = row == (channel // BLOCK) * kept + ((channel % BLOCK) // units) % kept
        for segment in range(segments):
            tile = got_ref[segment * units + unit].astype(jnp.float32)
            found.append(jnp.sum(jnp.where(wanted, tile, 0.0), axis=0, keepdims=True))
    lines = jnp.concatenate(found, axis=0).astype(jnp.bfloat16)
    swap = lax.broadcasted_iota(jnp.int32, (LANES, LANES), 0) + lax.broadcasted_iota(
        jnp.int32, (LANES, LANES), 1
    )
    swap = jnp.where(swap == LANES - 1, 1.0, 0.0).astype(jnp.bfloat16)
    for low in range(0, sample_count, LANES):
        high = sample_count - low
        out_ref[:, low : low + LANES] = jnp.dot(
            lines[:, high - LANES : high], swap, preferred_element_type=jnp.float32
        ).astype(out_ref.dtype)


def pick_sources(channels, got, units, kept, segments):
    count = PAIR_DEV * segments

    def body(*refs):
        pick_kernel(units, kept, segments, *refs)

    return pl.pallas_call(
        body,
        out_shape=pltpu.VMEM((count, got.shape[2]), jnp.bfloat16),
        in_specs=[
            pl.BlockSpec(memory_space=pltpu.SMEM),
            pl.BlockSpec(memory_space=pltpu.VMEM),
        ],
        out_specs=pl.BlockSpec(memory_space=pltpu.VMEM),
        name="pick_sources",
    )(in_scalar(channels), near_core(got))


def merge_in_kernel(got_ref, merged_ref, spread_ref, units):
    sample_count = merged_ref.shape[3]
    for segment in range(merged_ref.shape[1]):
        for chunk in range(sample_count // LANES):
            low = chunk * LANES
            tile = got_ref[segment * units : (segment + 1) * units, :, low : low + LANES]
            spread_ref[segment, chunk] = tile.astype(jnp.float32).reshape(units * 8, LANES)
            for block in range(2):
                rows = [
                    spread_ref[segment, chunk, pl.ds(block * 4 + place, units, stride=8), :]
                    for place in range(4)
                ]
                merged_ref[block, segment, :, low : low + LANES] = jnp.concatenate(
                    rows, axis=0
                ).astype(jnp.bfloat16)


def spread_like(segments, sample_count, units):
    return pltpu.VMEM((segments, sample_count // LANES, units * 8, LANES), jnp.float32)


def prepare_kernel(owned, units, merged_here, channel_ref, source_ref, *refs):
    if merged_here:
        own_ref, moved_ref, merged_ref, spread_ref = refs
        merge_in_kernel(own_ref, merged_ref, spread_ref, units)
    else:
        (moved_ref,) = refs
    segments = source_ref.shape[1] // PAIR_DEV
    spare = jnp.zeros((1, LANES), jnp.float32)
    for pair in range(PAIR_DEV):
        holder = (channel_ref[pair] % BLOCK) // owned
        for segment in range(segments):
            at = pair * segments + segment
            line = source_ref[holder, at : at + 1, :].astype(jnp.float32)
            line = jnp.concatenate([line, spare], axis=1)
            moved_ref[at] = toeplitz_rows(line, line.shape[1], 1).astype(jnp.bfloat16)


def prepare(channels, sources, own, owned, units):
    count, sample_count = sources.shape[1:]
    segments = count // PAIR_DEV
    out_shape = [pltpu.VMEM((count, LANES, sample_count + LANES), jnp.bfloat16)]
    scratch = []
    if own:
        merged = (NEAR // 2, segments, owned, sample_count)
        out_shape.append(pltpu.VMEM(merged, jnp.bfloat16))
        scratch.append(spread_like(segments, sample_count, units))

    def body(*refs):
        prepare_kernel(owned, units, bool(own), *refs)

    return pl.pallas_call(
        body,
        out_shape=out_shape,
        in_specs=[pl.BlockSpec(memory_space=pltpu.SMEM)]
        + [pl.BlockSpec(memory_space=pltpu.VMEM)] * (1 + len(own)),
        out_specs=[pl.BlockSpec(memory_space=pltpu.VMEM)] * len(out_shape),
        scratch_shapes=scratch,
        compiler_params=pltpu.CompilerParams(vmem_limit_bytes=KERNEL_VMEM),
        name="prepare",
    )(in_scalar(channels), near_core(sources), *map(near_core, own))


def lag_products(receivers, toeplitz):
    rows, sample_count = receivers[0].shape
    pieces = sample_count // LANES
    empty = jnp.zeros((rows, LANES), receivers[0].dtype)
    sides = []
    stacked = []
    pairs = []
    last = []
    for row, moved in zip(receivers, toeplitz, strict=True):
        parts = [row[:, i * LANES : (i + 1) * LANES] for i in range(pieces)]
        tiles = [
            moved[:, (pieces - i) * LANES : (pieces - i + 1) * LANES] for i in range(pieces + 1)
        ]
        sides.append(jnp.concatenate([empty, *parts], axis=0))
        sides.append(jnp.concatenate([*parts, empty], axis=0))
        stacked.append(jnp.concatenate(parts, axis=0))
        pairs.append(jnp.concatenate(tiles[0:pieces:2], axis=1))
        pairs.append(jnp.concatenate(tiles[1:pieces:2], axis=1))
        last.append(tiles[pieces])
    first = jnp.dot(
        jnp.concatenate(sides, axis=1),
        jnp.concatenate(pairs, axis=0),
        preferred_element_type=jnp.float32,
    )
    second = jnp.dot(
        jnp.concatenate(stacked, axis=1),
        jnp.concatenate(last, axis=0),
        preferred_element_type=jnp.float32,
    )
    sums = [None] * (2 * pieces)
    for i in range(pieces):
        sums[i] = second[i * rows : (i + 1) * rows]
    for column in range(pieces // 2):
        for i in range(pieces + 1):
            part = first[i * rows : (i + 1) * rows, column * LANES : (column + 1) * LANES]
            chunk = i - 1 + pieces - 2 * column
            sums[chunk] = part if sums[chunk] is None else sums[chunk] + part
    return sums


def correlate_kernel(units, merged_here, block_ref, moved_ref, *refs):
    if merged_here:
        own_ref, next_ref, out_hbm, out_ref, sems, after_ref, spread_ref = refs
        segments, _, sample_count = own_ref.shape[1:]
    else:
        merged_ref, out_hbm, out_ref, sems = refs
        segments, _, sample_count = merged_ref.shape[1:]
    factor = 1.0 / math.sqrt(sample_count * segments)
    if merged_here:
        merge_in_kernel(next_ref, after_ref, spread_ref, units)
    copies = []
    for pair in range(PAIR_DEV):
        block = block_ref[pair]
        if merged_here:
            ahead = block >= NEAR // 2
            place = block % (NEAR // 2)
            receivers = [
                jnp.where(ahead, after_ref[place, i], own_ref[place, i]) for i in range(segments)
            ]
        else:
            receivers = [merged_ref[block, i] for i in range(segments)]
        sums = lag_products(receivers, [moved_ref[pair * segments + i] for i in range(segments)])
        for chunk, part in enumerate(sums):
            out_ref[:, pair, chunk * LANES : (chunk + 1) * LANES] = part * factor
        copy = pltpu.make_async_copy(out_ref.at[:, pair], out_hbm.at[:, pair], sems.at[pair])
        copy.start()
        copies.append(copy)
    for copy in copies:
        copy.wait()


def correlate(chosen, toeplitz, receivers, owned, units):
    merged_here = len(receivers) == 2
    shape = (owned, PAIR_DEV, 2 * MAX_LAG)

    def body(*refs):
        correlate_kernel(units, merged_here, *refs)

    scratch = [
        pltpu.VMEM(shape, jnp.float32),
        pltpu.SemaphoreType.DMA((PAIR_DEV,)),
    ]
    if merged_here:
        own = receivers[0]
        scratch.append(pltpu.VMEM(own.shape, own.dtype))
        scratch.append(spread_like(own.shape[1], own.shape[3], units))
    return pl.pallas_call(
        body,
        out_shape=jax.ShapeDtypeStruct(shape, jnp.float32),
        in_specs=[pl.BlockSpec(memory_space=pltpu.SMEM)]
        + [pl.BlockSpec(memory_space=pltpu.VMEM)] * (1 + len(receivers)),
        out_specs=pl.BlockSpec(memory_space=pl.ANY),
        scratch_shapes=scratch,
        compiler_params=pltpu.CompilerParams(vmem_limit_bytes=KERNEL_VMEM),
        name="correlate",
    )(in_scalar(chosen), near_core(toeplitz), *map(near_core, receivers))


def local(recordings, gap_start, dropout_extent, filter_taps, source_channel, receiver_block):
    round_count, sample_count = recordings.shape[1], recordings.shape[3]
    segments = lax.axis_size("tm")
    units = lax.axis_size("chan")
    groups = units
    blocks = round_count * units // BLOCK
    near = blocks // groups
    owned = BLOCK // segments
    rounds_block = BLOCK // units
    slots = min(segments, rounds_block)
    kept = rounds_block // slots
    small = [x.reshape(1, x.size) for x in (filter_taps, gap_start, dropout_extent)]
    small += [source_channel, receiver_block]
    normalized, channels, chosen = normalize(recordings, small, blocks, slots, kept)
    sent = normalized.reshape(slots, groups, near * kept, sample_count)
    sent = jnp.repeat(sent, segments // slots, axis=0) if segments > slots else sent
    got = lax.all_to_all(
        sent.reshape(segments * groups, near * kept, sample_count),
        ("tm", "chan"),
        split_axis=0,
        concat_axis=0,
        tiled=True,
    )
    following = lax.ppermute(got, "chan", [(group, group - 1) for group in range(1, groups)])
    picked = pick_sources(channels, got, units, kept, segments)
    sources = lax.all_gather(picked, "tm")
    if kept == 4 and owned == 4 * units and near == 2:
        toeplitz, own = prepare(channels, sources, (got,), owned, units)
        return correlate(chosen, toeplitz, (own, following), owned, units)
    across = owned // kept
    first = lax.axis_index("tm") * owned % units
    apart = [x.reshape(segments, units, near, kept, sample_count) for x in (got, following)]
    apart = lax.dynamic_slice_in_dim(jnp.concatenate(apart, axis=2), first, across, axis=1)
    merged = apart.transpose(2, 0, 3, 1, 4).reshape(2 * near, segments, owned, sample_count)
    (toeplitz,) = prepare(channels, sources, (), owned, units)
    return correlate(chosen, toeplitz, (merged,), owned, units)


def solution(mesh):
    return jax.shard_map(
        local,
        mesh=mesh,
        in_specs=(
            P("tm", None, "chan", None),
            P("tm", None, "chan"),
            P("tm", None, "chan"),
            P(),
            P("chan"),
            P("chan"),
        ),
        out_specs=P("tm", "chan", None),
        check_vma=False,
    )
```

```python
import math

import jax
import jax.numpy as jnp
from jax import lax
from jax.experimental import pallas as pl
from jax.experimental.pallas import tpu as pltpu
from jax.sharding import PartitionSpec as P

BLOCK = 128
MAX_LAG = 512
PAIR_DEV = 4
LANES = 128
KERNEL_VMEM = 24 << 20
NEAR = 4


def near_core(x):
    return pltpu.with_memory_space_constraint(x, pltpu.VMEM)


def in_scalar(x):
    return pltpu.with_memory_space_constraint(x, pltpu.SMEM)


def toeplitz_rows(row, width, first=0):
    return pltpu.roll(
        jnp.broadcast_to(row, (LANES, width)), first, 1, stride=1, stride_axis=0
    )


def in_parts(x):
    first = x.astype(jnp.bfloat16)
    rest = x - first.astype(jnp.float32)
    second = rest.astype(jnp.bfloat16)
    return first, second, (rest - second.astype(jnp.float32)).astype(jnp.bfloat16)


def normalize_kernel(slots, kept, rec_hbm, *refs):
    small_refs, out_ref = refs[:5], refs[5]
    rec_ref, taps_ref, start_ref, extent_ref, sems = refs[8:]
    small_bufs = (taps_ref, start_ref, extent_ref, refs[6], refs[7])
    blocks = rec_hbm.shape[0]
    rows = blocks * kept
    pieces = rec_hbm.shape[2] // kept
    sample_count = pieces * LANES
    small = []
    for i, (small_ref, small_buf) in enumerate(zip(small_refs, small_bufs, strict=True)):
        copy = pltpu.make_async_copy(small_ref, small_buf, sems.at[slots + i])
        copy.start()
        small.append(copy)
    copies = []
    for slot in range(slots):
        copy = pltpu.make_async_copy(rec_hbm.at[:, slot], rec_ref.at[slot], sems.at[slot])
        copy.start()
        copies.append(copy)
    for copy in small:
        copy.wait()
    taps = jnp.concatenate([taps_ref[...], jnp.zeros((1, LANES), jnp.float32)], axis=1)
    w0, w1, w2 = in_parts(toeplitz_rows(taps, 2 * LANES))
    weights = jnp.concatenate([w0, w0, w0, w1, w1, w2], axis=0)
    starts = start_ref[...].astype(jnp.float32)
    ends = starts + extent_ref[...].astype(jnp.float32)
    round_count = starts.shape[1]
    lane = lax.broadcasted_iota(jnp.int32, (rows, round_count), 1)
    row = lax.broadcasted_iota(jnp.int32, (rows, round_count), 0)
    position = lax.broadcasted_iota(jnp.int32, (rows, LANES), 1).astype(jnp.float32)
    spans = []
    for slot in range(slots):
        own = lane == (row // kept) * (slots * kept) + slot * kept + row % kept
        start = jnp.sum(jnp.where(own, starts, 0.0), axis=1, keepdims=True)
        end = jnp.sum(jnp.where(own, ends, 0.0), axis=1, keepdims=True)
        spans.append((start, end, sample_count - (jnp.minimum(end, float(sample_count)) - start)))
    for copy in copies:
        copy.wait()
    for slot in range(slots):
        start, end, counted = spans[slot]
        flat = rec_ref.at[slot].reshape(rows * pieces, LANES)
        valids = []
        masked = []
        for piece in range(pieces):
            at = position + float(piece * LANES)
            valid = jnp.where((at >= start) & (at < end), 0.0, 1.0)
            valids.append(valid)
            masked.append(flat[pl.ds(piece, rows, stride=pieces), :] * valid)
        x0, x1, x2 = in_parts(jnp.concatenate(masked, axis=0))
        spread = jnp.dot(
            jnp.concatenate([x0, x1, x2, x0, x1, x0], axis=1),
            weights,
            preferred_element_type=jnp.float32,
        )
        kept_parts = []
        squares = jnp.zeros((rows, LANES), jnp.float32)
        for piece in range(pieces):
            filtered = spread[piece * rows : (piece + 1) * rows, :LANES]
            if piece:
                filtered = filtered + spread[(piece - 1) * rows : piece * rows, LANES:]
            filtered = filtered * valids[piece]
            squares = squares + filtered * filtered
            kept_parts.append(filtered)
        mean_square = jnp.sum(squares, axis=1, keepdims=True) / counted
        scale = lax.rsqrt(mean_square + 1e-05)
        normalized = jnp.concatenate(kept_parts, axis=1) * scale
        out_ref[slot] = normalized.astype(out_ref.dtype)


def normalize(recordings, small, blocks, slots, kept):
    sample_count = recordings.shape[3]
    pieces = sample_count // LANES
    view = recordings.reshape(blocks, slots, kept * pieces, LANES)

    def body(*refs):
        normalize_kernel(slots, kept, *refs)

    return pl.pallas_call(
        body,
        out_shape=(
            pltpu.VMEM((slots, blocks * kept, sample_count), jnp.bfloat16),
            pltpu.SMEM((PAIR_DEV,), jnp.int32),
            pltpu.SMEM((PAIR_DEV,), jnp.int32),
        ),
        in_specs=[pl.BlockSpec(memory_space=pl.ANY)] * (1 + len(small)),
        out_specs=[pl.BlockSpec(memory_space=pltpu.VMEM)]
        + [pl.BlockSpec(memory_space=pltpu.SMEM)] * 2,
        scratch_shapes=[
            pltpu.VMEM((slots, blocks, kept * pieces, LANES), jnp.float32),
            *[pltpu.VMEM(x.shape, x.dtype) for x in small[:3]],
            pltpu.SemaphoreType.DMA((slots + len(small),)),
        ],
        name="normalize",
    )(view, *small)


def pick_kernel(units, kept, segments, channel_ref, got_ref, out_ref):
    sample_count = got_ref.shape[2]
    shape = got_ref.shape[1:]
    row = lax.broadcasted_iota(jnp.int32, shape, 0)
    found = []
    for pair in range(PAIR_DEV):
        channel = channel_ref[pair]
        unit = channel % units
        wanted = row == (channel // BLOCK) * kept + ((channel % BLOCK) // units) % kept
        for segment in range(segments):
            tile = got_ref[segment * units + unit].astype(jnp.float32)
            found.append(jnp.sum(jnp.where(wanted, tile, 0.0), axis=0, keepdims=True))
    lines = jnp.concatenate(found, axis=0).astype(jnp.bfloat16)
    swap = lax.broadcasted_iota(jnp.int32, (LANES, LANES), 0) + lax.broadcasted_iota(
        jnp.int32, (LANES, LANES), 1
    )
    swap = jnp.where(swap == LANES - 1, 1.0, 0.0).astype(jnp.bfloat16)
    for low in range(0, sample_count, LANES):
        high = sample_count - low
        out_ref[:, low : low + LANES] = jnp.dot(
            lines[:, high - LANES : high], swap, preferred_element_type=jnp.float32
        ).astype(out_ref.dtype)


def pick_sources(channels, got, units, kept, segments):
    count = PAIR_DEV * segments

    def body(*refs):
        pick_kernel(units, kept, segments, *refs)

    return pl.pallas_call(
        body,
        out_shape=pltpu.VMEM((count, got.shape[2]), jnp.bfloat16),
        in_specs=[
            pl.BlockSpec(memory_space=pltpu.SMEM),
            pl.BlockSpec(memory_space=pltpu.VMEM),
        ],
        out_specs=pl.BlockSpec(memory_space=pltpu.VMEM),
        name="pick_sources",
    )(in_scalar(channels), near_core(got))


def merge_in_kernel(got_ref, merged_ref, spread_ref, units):
    sample_count = merged_ref.shape[3]
    for segment in range(merged_ref.shape[1]):
        for chunk in range(sample_count // LANES):
            low = chunk * LANES
            tile = got_ref[segment * units : (segment + 1) * units, :, low : low + LANES]
            spread_ref[segment, chunk] = tile.astype(jnp.float32).reshape(units * 8, LANES)
            for block in range(2):
                rows = [
                    spread_ref[segment, chunk, pl.ds(block * 4 + place, units, stride=8), :]
                    for place in range(4)
                ]
                merged_ref[block, segment, :, low : low + LANES] = jnp.concatenate(
                    rows, axis=0
                ).astype(jnp.bfloat16)


def spread_like(segments, sample_count, units):
    return pltpu.VMEM((segments, sample_count // LANES, units * 8, LANES), jnp.float32)


def prepare_kernel(owned, units, merged_here, channel_ref, source_ref, *refs):
    if merged_here:
        own_ref, moved_ref, merged_ref, spread_ref = refs
        merge_in_kernel(own_ref, merged_ref, spread_ref, units)
    else:
        (moved_ref,) = refs
    segments = source_ref.shape[1] // PAIR_DEV
    spare = jnp.zeros((1, LANES), jnp.float32)
    for pair in range(PAIR_DEV):
        holder = (channel_ref[pair] % BLOCK) // owned
        for segment in range(segments):
            at = pair * segments + segment
            line = source_ref[holder, at : at + 1, :].astype(jnp.float32)
            line = jnp.concatenate([line, spare], axis=1)
            moved_ref[at] = toeplitz_rows(line, line.shape[1], 1).astype(jnp.bfloat16)


def prepare(channels, sources, own, owned, units):
    count, sample_count = sources.shape[1:]
    segments = count // PAIR_DEV
    out_shape = [pltpu.VMEM((count, LANES, sample_count + LANES), jnp.bfloat16)]
    scratch = []
    if own:
        merged = (NEAR // 2, segments, owned, sample_count)
        out_shape.append(pltpu.VMEM(merged, jnp.bfloat16))
        scratch.append(spread_like(segments, sample_count, units))

    def body(*refs):
        prepare_kernel(owned, units, bool(own), *refs)

    return pl.pallas_call(
        body,
        out_shape=out_shape,
        in_specs=[pl.BlockSpec(memory_space=pltpu.SMEM)]
        + [pl.BlockSpec(memory_space=pltpu.VMEM)] * (1 + len(own)),
        out_specs=[pl.BlockSpec(memory_space=pltpu.VMEM)] * len(out_shape),
        scratch_shapes=scratch,
        compiler_params=pltpu.CompilerParams(vmem_limit_bytes=KERNEL_VMEM),
        name="prepare",
    )(in_scalar(channels), near_core(sources), *map(near_core, own))


def lag_products(receivers, toeplitz):
    rows, sample_count = receivers[0].shape
    pieces = sample_count // LANES
    empty = jnp.zeros((rows, LANES), receivers[0].dtype)
    sides = []
    stacked = []
    pairs = []
    last = []
    for row, moved in zip(receivers, toeplitz, strict=True):
        parts = [row[:, i * LANES : (i + 1) * LANES] for i in range(pieces)]
        tiles = [
            moved[:, (pieces - i) * LANES : (pieces - i + 1) * LANES] for i in range(pieces + 1)
        ]
        sides.append(jnp.concatenate([empty, *parts], axis=0))
        sides.append(jnp.concatenate([*parts, empty], axis=0))
        stacked.append(jnp.concatenate(parts, axis=0))
        pairs.append(jnp.concatenate(tiles[0:pieces:2], axis=1))
        pairs.append(jnp.concatenate(tiles[1:pieces:2], axis=1))
        last.append(tiles[pieces])
    first = jnp.dot(
        jnp.concatenate(sides, axis=1),
        jnp.concatenate(pairs, axis=0),
        preferred_element_type=jnp.float32,
    )
    second = jnp.dot(
        jnp.concatenate(stacked, axis=1),
        jnp.concatenate(last, axis=0),
        preferred_element_type=jnp.float32,
    )
    sums = [None] * (2 * pieces)
    for i in range(pieces):
        sums[i] = second[i * rows : (i + 1) * rows]
    for column in range(pieces // 2):
        for i in range(pieces + 1):
            part = first[i * rows : (i + 1) * rows, column * LANES : (column + 1) * LANES]
            chunk = i - 1 + pieces - 2 * column
            sums[chunk] = part if sums[chunk] is None else sums[chunk] + part
    return sums


def store_sums(out_ref, slot, sums, factor):
    for chunk, part in enumerate(sums):
        out_ref[:, slot, chunk * LANES : (chunk + 1) * LANES] = part * factor


def correlate_kernel(block_ref, moved_ref, merged_ref, out_hbm, out_ref, sems):
    blocks, segments, _, sample_count = merged_ref.shape
    factor = 1.0 / math.sqrt(sample_count * segments)
    copies = []
    for pair in range(PAIR_DEV):
        place = block_ref[pair] % blocks
        receivers = [merged_ref[place, i] for i in range(segments)]
        sums = lag_products(receivers, [moved_ref[pair * segments + i] for i in range(segments)])
        store_sums(out_ref, pair, sums, factor)
        copy = pltpu.make_async_copy(out_ref.at[:, pair], out_hbm.at[:, pair], sems.at[pair])
        copy.start()
        copies.append(copy)
    for copy in copies:
        copy.wait()


def correlate(chosen, toeplitz, merged):
    shape = (merged.shape[2], PAIR_DEV, 2 * MAX_LAG)
    return pl.pallas_call(
        correlate_kernel,
        out_shape=jax.ShapeDtypeStruct(shape, jnp.float32),
        in_specs=[
            pl.BlockSpec(memory_space=pltpu.SMEM),
            pl.BlockSpec(memory_space=pltpu.VMEM),
            pl.BlockSpec(memory_space=pltpu.VMEM),
        ],
        out_specs=pl.BlockSpec(memory_space=pl.ANY),
        scratch_shapes=[
            pltpu.VMEM(shape, jnp.float32),
            pltpu.SemaphoreType.DMA((PAIR_DEV,)),
        ],
        compiler_params=pltpu.CompilerParams(vmem_limit_bytes=KERNEL_VMEM),
        name="correlate",
    )(in_scalar(chosen), near_core(toeplitz), near_core(merged))


def ahead_kernel(
    units, block_ref, moved_ref, next_ref, old_hbm, out_hbm, order_ref, after_ref, spread_ref, out_ref, sems
):
    blocks, segments, _, sample_count = after_ref.shape
    factor = 1.0 / math.sqrt(sample_count * segments)
    count = jnp.int32(0)
    for pair in range(PAIR_DEV):
        order_ref[count] = pair
        count = count + jnp.where(block_ref[pair] >= blocks, 1, 0)

    @pl.when(count > 0)
    def _():
        merge_in_kernel(next_ref, after_ref, spread_ref, units)

    for first in range(0, PAIR_DEV, 2):

        @pl.when(count > first)
        def _(first=first):
            for slot in (first, first + 1):
                pair = order_ref[jnp.minimum(slot, count - 1)]
                place = block_ref[pair] - blocks
                receivers = [after_ref[place, i] for i in range(segments)]
                moved = [moved_ref[pair * segments + i] for i in range(segments)]
                store_sums(out_ref, slot, lag_products(receivers, moved), factor)

            for slot in (first, first + 1):
                for pair in range(PAIR_DEV):

                    @pl.when((count > slot) & (order_ref[jnp.minimum(slot, count - 1)] == pair))
                    def _(slot=slot, pair=pair):
                        pltpu.make_async_copy(
                            out_ref.at[:, slot], out_hbm.at[:, pair], sems.at[slot]
                        ).start()

    for slot in range(PAIR_DEV):

        @pl.when(count > slot)
        def _(slot=slot):
            pltpu.make_async_copy(out_ref.at[:, slot], out_hbm.at[:, slot], sems.at[slot]).wait()


def correlate_ahead(chosen, toeplitz, following, stacks, units):
    owned, segments, sample_count = 4 * units, following.shape[0] // units, following.shape[2]

    def body(*refs):
        ahead_kernel(units, *refs)

    return pl.pallas_call(
        body,
        out_shape=jax.ShapeDtypeStruct(stacks.shape, stacks.dtype),
        in_specs=[
            pl.BlockSpec(memory_space=pltpu.SMEM),
            pl.BlockSpec(memory_space=pltpu.VMEM),
            pl.BlockSpec(memory_space=pltpu.VMEM),
            pl.BlockSpec(memory_space=pl.ANY),
        ],
        out_specs=pl.BlockSpec(memory_space=pl.ANY),
        scratch_shapes=[
            pltpu.SMEM((PAIR_DEV,), jnp.int32),
            pltpu.VMEM((NEAR // 2, segments, owned, sample_count), jnp.bfloat16),
            spread_like(segments, sample_count, units),
            pltpu.VMEM(stacks.shape, stacks.dtype),
            pltpu.SemaphoreType.DMA((PAIR_DEV,)),
        ],
        input_output_aliases={3: 0},
        compiler_params=pltpu.CompilerParams(vmem_limit_bytes=KERNEL_VMEM),
        name="correlate_ahead",
    )(in_scalar(chosen), near_core(toeplitz), near_core(following), stacks)


def local(recordings, gap_start, dropout_extent, filter_taps, source_channel, receiver_block):
    round_count, sample_count = recordings.shape[1], recordings.shape[3]
    segments = lax.axis_size("tm")
    units = lax.axis_size("chan")
    groups = units
    blocks = round_count * units // BLOCK
    near = blocks // groups
    owned = BLOCK // segments
    rounds_block = BLOCK // units
    slots = min(segments, rounds_block)
    kept = rounds_block // slots
    small = [x.reshape(1, x.size) for x in (filter_taps, gap_start, dropout_extent)]
    small += [source_channel, receiver_block]
    normalized, channels, chosen = normalize(recordings, small, blocks, slots, kept)
    sent = normalized.reshape(slots, groups, near * kept, sample_count)
    sent = jnp.repeat(sent, segments // slots, axis=0) if segments > slots else sent
    got = lax.all_to_all(
        sent.reshape(segments * groups, near * kept, sample_count),
        ("tm", "chan"),
        split_axis=0,
        concat_axis=0,
        tiled=True,
    )
    following = lax.ppermute(got, "chan", [(group, group - 1) for group in range(1, groups)])
    picked = pick_sources(channels, got, units, kept, segments)
    sources = lax.all_gather(picked, "tm")
    if kept == 4 and owned == 4 * units and near == 2:
        toeplitz, own = prepare(channels, sources, (got,), owned, units)
        stacks = correlate(chosen, toeplitz, own)
        return correlate_ahead(chosen, toeplitz, following, stacks, units)
    across = owned // kept
    first = lax.axis_index("tm") * owned % units
    apart = [x.reshape(segments, units, near, kept, sample_count) for x in (got, following)]
    apart = lax.dynamic_slice_in_dim(jnp.concatenate(apart, axis=2), first, across, axis=1)
    merged = apart.transpose(2, 0, 3, 1, 4).reshape(2 * near, segments, owned, sample_count)
    (toeplitz,) = prepare(channels, sources, (), owned, units)
    return correlate(chosen, toeplitz, merged)


def solution(mesh):
    return jax.shard_map(
        local,
        mesh=mesh,
        in_specs=(
            P("tm", None, "chan", None),
            P("tm", None, "chan"),
            P("tm", None, "chan"),
            P(),
            P("chan"),
            P("chan"),
        ),
        out_specs=P("tm", "chan", None),
        check_vma=False,
    )
```

```python
import math

import jax
import jax.numpy as jnp
from jax import lax
from jax.experimental import pallas as pl
from jax.experimental.pallas import tpu as pltpu
from jax.sharding import PartitionSpec as P

BLOCK = 128
MAX_LAG = 512
PAIR_DEV = 4
LANES = 128
KERNEL_VMEM = 24 << 20
NEAR = 4


def near_core(x):
    return pltpu.with_memory_space_constraint(x, pltpu.VMEM)


def in_scalar(x):
    return pltpu.with_memory_space_constraint(x, pltpu.SMEM)


def toeplitz_rows(row, width, first=0):
    return pltpu.roll(
        jnp.broadcast_to(row, (LANES, width)), first, 1, stride=1, stride_axis=0
    )


def in_parts(x):
    first = x.astype(jnp.bfloat16)
    rest = x - first.astype(jnp.float32)
    second = rest.astype(jnp.bfloat16)
    return first, second, (rest - second.astype(jnp.float32)).astype(jnp.bfloat16)


def normalize_kernel(slots, kept, rec_hbm, *refs):
    small_refs, out_ref = refs[:5], refs[5]
    rec_ref, taps_ref, start_ref, extent_ref, sems = refs[8:]
    small_bufs = (taps_ref, start_ref, extent_ref, refs[6], refs[7])
    blocks = rec_hbm.shape[0]
    rows = blocks * kept
    pieces = rec_hbm.shape[2] // kept
    sample_count = pieces * LANES
    small = []
    for i, (small_ref, small_buf) in enumerate(zip(small_refs, small_bufs, strict=True)):
        copy = pltpu.make_async_copy(small_ref, small_buf, sems.at[slots + i])
        copy.start()
        small.append(copy)
    copies = []
    for slot in range(slots):
        copy = pltpu.make_async_copy(rec_hbm.at[:, slot], rec_ref.at[slot], sems.at[slot])
        copy.start()
        copies.append(copy)
    for copy in small:
        copy.wait()
    taps = jnp.concatenate([taps_ref[...], jnp.zeros((1, LANES), jnp.float32)], axis=1)
    w0, w1, w2 = in_parts(toeplitz_rows(taps, 2 * LANES))
    weights = jnp.concatenate([w0, w0, w0, w1, w1, w2], axis=0)
    starts = start_ref[...].astype(jnp.float32)
    ends = starts + extent_ref[...].astype(jnp.float32)
    round_count = starts.shape[1]
    lane = lax.broadcasted_iota(jnp.int32, (rows, round_count), 1)
    row = lax.broadcasted_iota(jnp.int32, (rows, round_count), 0)
    position = lax.broadcasted_iota(jnp.int32, (rows, LANES), 1).astype(jnp.float32)
    spans = []
    for slot in range(slots):
        own = lane == (row // kept) * (slots * kept) + slot * kept + row % kept
        start = jnp.sum(jnp.where(own, starts, 0.0), axis=1, keepdims=True)
        end = jnp.sum(jnp.where(own, ends, 0.0), axis=1, keepdims=True)
        spans.append((start, end, sample_count - (jnp.minimum(end, float(sample_count)) - start)))
    for copy in copies:
        copy.wait()
    for slot in range(slots):
        start, end, counted = spans[slot]
        flat = rec_ref.at[slot].reshape(rows * pieces, LANES)
        valids = []
        masked = []
        for piece in range(pieces):
            at = position + float(piece * LANES)
            valid = jnp.where((at >= start) & (at < end), 0.0, 1.0)
            valids.append(valid)
            masked.append(flat[pl.ds(piece, rows, stride=pieces), :] * valid)
        x0, x1, x2 = in_parts(jnp.concatenate(masked, axis=0))
        spread = jnp.dot(
            jnp.concatenate([x0, x1, x2, x0, x1, x0], axis=1),
            weights,
            preferred_element_type=jnp.float32,
        )
        kept_parts = []
        squares = jnp.zeros((rows, LANES), jnp.float32)
        for piece in range(pieces):
            filtered = spread[piece * rows : (piece + 1) * rows, :LANES]
            if piece:
                filtered = filtered + spread[(piece - 1) * rows : piece * rows, LANES:]
            filtered = filtered * valids[piece]
            squares = squares + filtered * filtered
            kept_parts.append(filtered)
        mean_square = jnp.sum(squares, axis=1, keepdims=True) / counted
        scale = lax.rsqrt(mean_square + 1e-05)
        normalized = jnp.concatenate(kept_parts, axis=1) * scale
        out_ref[slot] = normalized.astype(out_ref.dtype)


def normalize(recordings, small, blocks, slots, kept):
    sample_count = recordings.shape[3]
    pieces = sample_count // LANES
    view = recordings.reshape(blocks, slots, kept * pieces, LANES)

    def body(*refs):
        normalize_kernel(slots, kept, *refs)

    return pl.pallas_call(
        body,
        out_shape=(
            pltpu.VMEM((slots, blocks * kept, sample_count), jnp.bfloat16),
            pltpu.SMEM((PAIR_DEV,), jnp.int32),
            pltpu.SMEM((PAIR_DEV,), jnp.int32),
        ),
        in_specs=[pl.BlockSpec(memory_space=pl.ANY)] * (1 + len(small)),
        out_specs=[pl.BlockSpec(memory_space=pltpu.VMEM)]
        + [pl.BlockSpec(memory_space=pltpu.SMEM)] * 2,
        scratch_shapes=[
            pltpu.VMEM((slots, blocks, kept * pieces, LANES), jnp.float32),
            *[pltpu.VMEM(x.shape, x.dtype) for x in small[:3]],
            pltpu.SemaphoreType.DMA((slots + len(small),)),
        ],
        name="normalize",
    )(view, *small)


def pick_kernel(units, kept, segments, channel_ref, got_ref, out_ref):
    sample_count = got_ref.shape[2]
    shape = got_ref.shape[1:]
    row = lax.broadcasted_iota(jnp.int32, shape, 0)
    found = []
    for pair in range(PAIR_DEV):
        channel = channel_ref[pair]
        unit = channel % units
        wanted = row == (channel // BLOCK) * kept + ((channel % BLOCK) // units) % kept
        for segment in range(segments):
            tile = got_ref[segment * units + unit].astype(jnp.float32)
            found.append(jnp.sum(jnp.where(wanted, tile, 0.0), axis=0, keepdims=True))
    lines = jnp.concatenate(found, axis=0).astype(jnp.bfloat16)
    swap = lax.broadcasted_iota(jnp.int32, (LANES, LANES), 0) + lax.broadcasted_iota(
        jnp.int32, (LANES, LANES), 1
    )
    swap = jnp.where(swap == LANES - 1, 1.0, 0.0).astype(jnp.bfloat16)
    for low in range(0, sample_count, LANES):
        high = sample_count - low
        out_ref[:, low : low + LANES] = jnp.dot(
            lines[:, high - LANES : high], swap, preferred_element_type=jnp.float32
        ).astype(out_ref.dtype)


def pick_sources(channels, got, units, kept, segments):
    count = PAIR_DEV * segments

    def body(*refs):
        pick_kernel(units, kept, segments, *refs)

    return pl.pallas_call(
        body,
        out_shape=pltpu.VMEM((count, got.shape[2]), jnp.bfloat16),
        in_specs=[
            pl.BlockSpec(memory_space=pltpu.SMEM),
            pl.BlockSpec(memory_space=pltpu.VMEM),
        ],
        out_specs=pl.BlockSpec(memory_space=pltpu.VMEM),
        name="pick_sources",
    )(in_scalar(channels), near_core(got))


def merge_in_kernel(got_ref, merged_ref, spread_ref, units):
    sample_count = merged_ref.shape[3]
    for segment in range(merged_ref.shape[1]):
        for chunk in range(sample_count // LANES):
            low = chunk * LANES
            tile = got_ref[segment * units : (segment + 1) * units, :, low : low + LANES]
            spread_ref[segment, chunk] = tile.astype(jnp.float32).reshape(units * 8, LANES)
            for block in range(2):
                rows = [
                    spread_ref[segment, chunk, pl.ds(block * 4 + place, units, stride=8), :]
                    for place in range(4)
                ]
                merged_ref[block, segment, :, low : low + LANES] = jnp.concatenate(
                    rows, axis=0
                ).astype(jnp.bfloat16)


def spread_like(segments, sample_count, units):
    return pltpu.VMEM((segments, sample_count // LANES, units * 8, LANES), jnp.float32)


def prepare_kernel(owned, units, merged_here, channel_ref, source_ref, *refs):
    if merged_here:
        own_ref, moved_ref, merged_ref, spread_ref = refs
        merge_in_kernel(own_ref, merged_ref, spread_ref, units)
    else:
        (moved_ref,) = refs
    segments = source_ref.shape[1] // PAIR_DEV
    spare = jnp.zeros((1, LANES), jnp.float32)
    for pair in range(PAIR_DEV):
        holder = (channel_ref[pair] % BLOCK) // owned
        for segment in range(segments):
            at = pair * segments + segment
            line = source_ref[holder, at : at + 1, :].astype(jnp.float32)
            line = jnp.concatenate([line, spare], axis=1)
            moved_ref[at] = toeplitz_rows(line, line.shape[1], 1).astype(jnp.bfloat16)


def prepare(channels, sources, own, owned, units):
    count, sample_count = sources.shape[1:]
    segments = count // PAIR_DEV
    out_shape = [pltpu.VMEM((count, LANES, sample_count + LANES), jnp.bfloat16)]
    scratch = []
    if own:
        merged = (NEAR // 2, segments, owned, sample_count)
        out_shape.append(pltpu.VMEM(merged, jnp.bfloat16))
        scratch.append(spread_like(segments, sample_count, units))

    def body(*refs):
        prepare_kernel(owned, units, bool(own), *refs)

    return pl.pallas_call(
        body,
        out_shape=out_shape,
        in_specs=[pl.BlockSpec(memory_space=pltpu.SMEM)]
        + [pl.BlockSpec(memory_space=pltpu.VMEM)] * (1 + len(own)),
        out_specs=[pl.BlockSpec(memory_space=pltpu.VMEM)] * len(out_shape),
        scratch_shapes=scratch,
        compiler_params=pltpu.CompilerParams(vmem_limit_bytes=KERNEL_VMEM),
        name="prepare",
    )(in_scalar(channels), near_core(sources), *map(near_core, own))


def lag_products(receivers, toeplitz):
    rows, sample_count = receivers[0].shape
    pieces = sample_count // LANES
    empty = jnp.zeros((rows, LANES), receivers[0].dtype)
    sides = []
    stacked = []
    pairs = []
    last = []
    for row, moved in zip(receivers, toeplitz, strict=True):
        parts = [row[:, i * LANES : (i + 1) * LANES] for i in range(pieces)]
        tiles = [
            moved[:, (pieces - i) * LANES : (pieces - i + 1) * LANES] for i in range(pieces + 1)
        ]
        sides.append(jnp.concatenate([empty, *parts], axis=0))
        sides.append(jnp.concatenate([*parts, empty], axis=0))
        stacked.append(jnp.concatenate(parts, axis=0))
        pairs.append(jnp.concatenate(tiles[0:pieces:2], axis=1))
        pairs.append(jnp.concatenate(tiles[1:pieces:2], axis=1))
        last.append(tiles[pieces])
    first = jnp.dot(
        jnp.concatenate(sides, axis=1),
        jnp.concatenate(pairs, axis=0),
        preferred_element_type=jnp.float32,
    )
    second = jnp.dot(
        jnp.concatenate(stacked, axis=1),
        jnp.concatenate(last, axis=0),
        preferred_element_type=jnp.float32,
    )
    sums = [None] * (2 * pieces)
    for i in range(pieces):
        sums[i] = second[i * rows : (i + 1) * rows]
    for column in range(pieces // 2):
        for i in range(pieces + 1):
            part = first[i * rows : (i + 1) * rows, column * LANES : (column + 1) * LANES]
            chunk = i - 1 + pieces - 2 * column
            sums[chunk] = part if sums[chunk] is None else sums[chunk] + part
    return sums


def correlate_kernel(units, merged_here, block_ref, moved_ref, *refs):
    if merged_here:
        own_ref, next_ref, out_hbm, out_ref, sems, after_ref, spread_ref = refs
        segments, _, sample_count = own_ref.shape[1:]
    else:
        merged_ref, out_hbm, out_ref, sems = refs
        segments, _, sample_count = merged_ref.shape[1:]
    factor = 1.0 / math.sqrt(sample_count * segments)
    if merged_here:
        merge_in_kernel(next_ref, after_ref, spread_ref, units)
    every = []
    for pair in range(PAIR_DEV):
        block = block_ref[pair]
        if merged_here:
            ahead = block >= NEAR // 2
            place = block % (NEAR // 2)
            receivers = [
                jnp.where(ahead, after_ref[place, i], own_ref[place, i]) for i in range(segments)
            ]
        else:
            receivers = [merged_ref[block, i] for i in range(segments)]
        moved = [moved_ref[pair * segments + i] for i in range(segments)]
        every.append(lag_products(receivers, moved))
    chunks, places, _ = out_ref.shape
    owned = places // PAIR_DEV
    copies = []
    for chunk in range(chunks):
        for pair in range(PAIR_DEV):
            out_ref[chunk, pl.ds(pair, owned, stride=PAIR_DEV), :] = every[pair][chunk] * factor
        copy = pltpu.make_async_copy(
            out_ref.at[chunk].reshape(owned, PAIR_DEV, LANES),
            out_hbm.at[:, :, chunk * LANES : (chunk + 1) * LANES],
            sems.at[chunk],
        )
        copy.start()
        copies.append(copy)
    for copy in copies:
        copy.wait()


def correlate(chosen, toeplitz, receivers, owned, units):
    merged_here = len(receivers) == 2
    shape = (owned, PAIR_DEV, 2 * MAX_LAG)
    chunks = 2 * MAX_LAG // LANES

    def body(*refs):
        correlate_kernel(units, merged_here, *refs)

    scratch = [
        pltpu.VMEM((chunks, owned * PAIR_DEV, LANES), jnp.float32),
        pltpu.SemaphoreType.DMA((chunks,)),
    ]
    if merged_here:
        own = receivers[0]
        scratch.append(pltpu.VMEM(own.shape, own.dtype))
        scratch.append(spread_like(own.shape[1], own.shape[3], units))
    return pl.pallas_call(
        body,
        out_shape=jax.ShapeDtypeStruct(shape, jnp.float32),
        in_specs=[pl.BlockSpec(memory_space=pltpu.SMEM)]
        + [pl.BlockSpec(memory_space=pltpu.VMEM)] * (1 + len(receivers)),
        out_specs=pl.BlockSpec(memory_space=pl.ANY),
        scratch_shapes=scratch,
        compiler_params=pltpu.CompilerParams(vmem_limit_bytes=KERNEL_VMEM),
        name="correlate",
    )(in_scalar(chosen), near_core(toeplitz), *map(near_core, receivers))


def local(recordings, gap_start, dropout_extent, filter_taps, source_channel, receiver_block):
    round_count, sample_count = recordings.shape[1], recordings.shape[3]
    segments = lax.axis_size("tm")
    units = lax.axis_size("chan")
    groups = units
    blocks = round_count * units // BLOCK
    near = blocks // groups
    owned = BLOCK // segments
    rounds_block = BLOCK // units
    slots = min(segments, rounds_block)
    kept = rounds_block // slots
    small = [x.reshape(1, x.size) for x in (filter_taps, gap_start, dropout_extent)]
    small += [source_channel, receiver_block]
    normalized, channels, chosen = normalize(recordings, small, blocks, slots, kept)
    sent = normalized.reshape(slots, groups, near * kept, sample_count)
    sent = jnp.repeat(sent, segments // slots, axis=0) if segments > slots else sent
    got = lax.all_to_all(
        sent.reshape(segments * groups, near * kept, sample_count),
        ("tm", "chan"),
        split_axis=0,
        concat_axis=0,
        tiled=True,
    )
    following = lax.ppermute(got, "chan", [(group, group - 1) for group in range(1, groups)])
    picked = pick_sources(channels, got, units, kept, segments)
    sources = lax.all_gather(picked, "tm")
    if kept == 4 and owned == 4 * units and near == 2:
        toeplitz, own = prepare(channels, sources, (got,), owned, units)
        return correlate(chosen, toeplitz, (own, following), owned, units)
    across = owned // kept
    first = lax.axis_index("tm") * owned % units
    apart = [x.reshape(segments, units, near, kept, sample_count) for x in (got, following)]
    apart = lax.dynamic_slice_in_dim(jnp.concatenate(apart, axis=2), first, across, axis=1)
    merged = apart.transpose(2, 0, 3, 1, 4).reshape(2 * near, segments, owned, sample_count)
    (toeplitz,) = prepare(channels, sources, (), owned, units)
    return correlate(chosen, toeplitz, (merged,), owned, units)


def solution(mesh):
    return jax.shard_map(
        local,
        mesh=mesh,
        in_specs=(
            P("tm", None, "chan", None),
            P("tm", None, "chan"),
            P("tm", None, "chan"),
            P(),
            P("chan"),
            P("chan"),
        ),
        out_specs=P("tm", "chan", None),
        check_vma=False,
    )
```

```python
import math

import jax
import jax.numpy as jnp
from jax import lax
from jax.experimental import pallas as pl
from jax.experimental.pallas import tpu as pltpu
from jax.sharding import PartitionSpec as P

BLOCK = 128
MAX_LAG = 512
PAIR_DEV = 4
LANES = 128
KERNEL_VMEM = 24 << 20
NEAR = 4


def near_core(x):
    return pltpu.with_memory_space_constraint(x, pltpu.VMEM)


def in_scalar(x):
    return pltpu.with_memory_space_constraint(x, pltpu.SMEM)


def toeplitz_rows(row, width, first=0):
    return pltpu.roll(
        jnp.broadcast_to(row, (LANES, width)), first, 1, stride=1, stride_axis=0
    )


def in_parts(x):
    first = x.astype(jnp.bfloat16)
    rest = x - first.astype(jnp.float32)
    second = rest.astype(jnp.bfloat16)
    return first, second, (rest - second.astype(jnp.float32)).astype(jnp.bfloat16)


def normalize_kernel(slots, kept, rec_hbm, *refs):
    small_refs, out_ref = refs[:5], refs[5]
    rec_ref, taps_ref, start_ref, extent_ref, sems = refs[8:]
    small_bufs = (taps_ref, start_ref, extent_ref, refs[6], refs[7])
    blocks = rec_hbm.shape[0]
    rows = blocks * kept
    pieces = rec_hbm.shape[2] // kept
    sample_count = pieces * LANES
    small = []
    for i, (small_ref, small_buf) in enumerate(zip(small_refs, small_bufs, strict=True)):
        copy = pltpu.make_async_copy(small_ref, small_buf, sems.at[slots + i])
        copy.start()
        small.append(copy)
    copies = []
    for slot in range(slots):
        copy = pltpu.make_async_copy(rec_hbm.at[:, slot], rec_ref.at[slot], sems.at[slot])
        copy.start()
        copies.append(copy)
    for copy in small:
        copy.wait()
    taps = jnp.concatenate([taps_ref[...], jnp.zeros((1, LANES), jnp.float32)], axis=1)
    w0, w1, w2 = in_parts(toeplitz_rows(taps, 2 * LANES))
    weights = jnp.concatenate([w0, w0, w0, w1, w1, w2], axis=0)
    starts = start_ref[...].astype(jnp.float32)
    ends = starts + extent_ref[...].astype(jnp.float32)
    round_count = starts.shape[1]
    lane = lax.broadcasted_iota(jnp.int32, (rows, round_count), 1)
    row = lax.broadcasted_iota(jnp.int32, (rows, round_count), 0)
    position = lax.broadcasted_iota(jnp.int32, (rows, LANES), 1).astype(jnp.float32)
    spans = []
    for slot in range(slots):
        own = lane == (row // kept) * (slots * kept) + slot * kept + row % kept
        start = jnp.sum(jnp.where(own, starts, 0.0), axis=1, keepdims=True)
        end = jnp.sum(jnp.where(own, ends, 0.0), axis=1, keepdims=True)
        spans.append((start, end, sample_count - (jnp.minimum(end, float(sample_count)) - start)))
    for copy in copies:
        copy.wait()
    for slot in range(slots):
        start, end, counted = spans[slot]
        flat = rec_ref.at[slot].reshape(rows * pieces, LANES)
        valids = []
        masked = []
        for piece in range(pieces):
            at = position + float(piece * LANES)
            valid = jnp.where((at >= start) & (at < end), 0.0, 1.0)
            valids.append(valid)
            masked.append(flat[pl.ds(piece, rows, stride=pieces), :] * valid)
        x0, x1, x2 = in_parts(jnp.concatenate(masked, axis=0))
        spread = jnp.dot(
            jnp.concatenate([x0, x1, x2, x0, x1, x0], axis=1),
            weights,
            preferred_element_type=jnp.float32,
        )
        kept_parts = []
        squares = jnp.zeros((rows, LANES), jnp.float32)
        for piece in range(pieces):
            filtered = spread[piece * rows : (piece + 1) * rows, :LANES]
            if piece:
                filtered = filtered + spread[(piece - 1) * rows : piece * rows, LANES:]
            filtered = filtered * valids[piece]
            squares = squares + filtered * filtered
            kept_parts.append(filtered)
        mean_square = jnp.sum(squares, axis=1, keepdims=True) / counted
        scale = lax.rsqrt(mean_square + 1e-05)
        normalized = jnp.concatenate(kept_parts, axis=1) * scale
        out_ref[slot] = normalized.astype(out_ref.dtype)


def normalize(recordings, small, blocks, slots, kept):
    sample_count = recordings.shape[3]
    pieces = sample_count // LANES
    view = recordings.reshape(blocks, slots, kept * pieces, LANES)

    def body(*refs):
        normalize_kernel(slots, kept, *refs)

    return pl.pallas_call(
        body,
        out_shape=(
            pltpu.VMEM((slots, blocks * kept, sample_count), jnp.bfloat16),
            pltpu.SMEM((PAIR_DEV,), jnp.int32),
            pltpu.SMEM((PAIR_DEV,), jnp.int32),
        ),
        in_specs=[pl.BlockSpec(memory_space=pl.ANY)] * (1 + len(small)),
        out_specs=[pl.BlockSpec(memory_space=pltpu.VMEM)]
        + [pl.BlockSpec(memory_space=pltpu.SMEM)] * 2,
        scratch_shapes=[
            pltpu.VMEM((slots, blocks, kept * pieces, LANES), jnp.float32),
            *[pltpu.VMEM(x.shape, x.dtype) for x in small[:3]],
            pltpu.SemaphoreType.DMA((slots + len(small),)),
        ],
        name="normalize",
    )(view, *small)


def pick_kernel(units, kept, segments, channel_ref, got_ref, out_ref):
    sample_count = got_ref.shape[2]
    shape = got_ref.shape[1:]
    row = lax.broadcasted_iota(jnp.int32, shape, 0)
    found = []
    for pair in range(PAIR_DEV):
        channel = channel_ref[pair]
        unit = channel % units
        wanted = row == (channel // BLOCK) * kept + ((channel % BLOCK) // units) % kept
        for segment in range(segments):
            tile = got_ref[segment * units + unit].astype(jnp.float32)
            found.append(jnp.sum(jnp.where(wanted, tile, 0.0), axis=0, keepdims=True))
    lines = jnp.concatenate(found, axis=0).astype(jnp.bfloat16)
    swap = lax.broadcasted_iota(jnp.int32, (LANES, LANES), 0) + lax.broadcasted_iota(
        jnp.int32, (LANES, LANES), 1
    )
    swap = jnp.where(swap == LANES - 1, 1.0, 0.0).astype(jnp.bfloat16)
    for low in range(0, sample_count, LANES):
        high = sample_count - low
        out_ref[:, low : low + LANES] = jnp.dot(
            lines[:, high - LANES : high], swap, preferred_element_type=jnp.float32
        ).astype(out_ref.dtype)


def pick_sources(channels, got, units, kept, segments):
    count = PAIR_DEV * segments

    def body(*refs):
        pick_kernel(units, kept, segments, *refs)

    return pl.pallas_call(
        body,
        out_shape=pltpu.VMEM((count, got.shape[2]), jnp.bfloat16),
        in_specs=[
            pl.BlockSpec(memory_space=pltpu.SMEM),
            pl.BlockSpec(memory_space=pltpu.VMEM),
        ],
        out_specs=pl.BlockSpec(memory_space=pltpu.VMEM),
        name="pick_sources",
    )(in_scalar(channels), near_core(got))


def merge_in_kernel(got_ref, merged_ref, spread_ref, units):
    sample_count = merged_ref.shape[3]
    for segment in range(merged_ref.shape[1]):
        for chunk in range(sample_count // LANES):
            low = chunk * LANES
            tile = got_ref[segment * units : (segment + 1) * units, :, low : low + LANES]
            spread_ref[segment, chunk] = tile.astype(jnp.float32).reshape(units * 8, LANES)
            for block in range(2):
                rows = [
                    spread_ref[segment, chunk, pl.ds(block * 4 + place, units, stride=8), :]
                    for place in range(4)
                ]
                merged_ref[block, segment, :, low : low + LANES] = jnp.concatenate(
                    rows, axis=0
                ).astype(jnp.bfloat16)


def spread_like(segments, sample_count, units):
    return pltpu.VMEM((segments, sample_count // LANES, units * 8, LANES), jnp.float32)


def prepare_kernel(owned, units, merged_here, channel_ref, source_ref, *refs):
    if merged_here:
        own_ref, moved_ref, merged_ref, spread_ref = refs
        merge_in_kernel(own_ref, merged_ref, spread_ref, units)
    else:
        (moved_ref,) = refs
    segments = source_ref.shape[1] // PAIR_DEV
    spare = jnp.zeros((1, LANES), jnp.float32)
    for pair in range(PAIR_DEV):
        holder = (channel_ref[pair] % BLOCK) // owned
        for segment in range(segments):
            at = pair * segments + segment
            line = source_ref[holder, at : at + 1, :].astype(jnp.float32)
            line = jnp.concatenate([line, spare], axis=1)
            moved_ref[at] = toeplitz_rows(line, line.shape[1], 1).astype(jnp.bfloat16)


def prepare(channels, sources, own, owned, units):
    count, sample_count = sources.shape[1:]
    segments = count // PAIR_DEV
    out_shape = [pltpu.VMEM((count, LANES, sample_count + LANES), jnp.bfloat16)]
    scratch = []
    if own:
        merged = (NEAR // 2, segments, owned, sample_count)
        out_shape.append(pltpu.VMEM(merged, jnp.bfloat16))
        scratch.append(spread_like(segments, sample_count, units))

    def body(*refs):
        prepare_kernel(owned, units, bool(own), *refs)

    return pl.pallas_call(
        body,
        out_shape=out_shape,
        in_specs=[pl.BlockSpec(memory_space=pltpu.SMEM)]
        + [pl.BlockSpec(memory_space=pltpu.VMEM)] * (1 + len(own)),
        out_specs=[pl.BlockSpec(memory_space=pltpu.VMEM)] * len(out_shape),
        scratch_shapes=scratch,
        compiler_params=pltpu.CompilerParams(vmem_limit_bytes=KERNEL_VMEM),
        name="prepare",
    )(in_scalar(channels), near_core(sources), *map(near_core, own))


def lag_products(receivers, toeplitz):
    rows, sample_count = receivers[0].shape
    pieces = sample_count // LANES
    empty = jnp.zeros((rows, LANES), receivers[0].dtype)
    sides = []
    stacked = []
    pairs = []
    last = []
    for row, moved in zip(receivers, toeplitz, strict=True):
        parts = [row[:, i * LANES : (i + 1) * LANES] for i in range(pieces)]
        tiles = [
            moved[:, (pieces - i) * LANES : (pieces - i + 1) * LANES] for i in range(pieces + 1)
        ]
        sides.append(jnp.concatenate([empty, *parts], axis=0))
        sides.append(jnp.concatenate([*parts, empty], axis=0))
        stacked.append(jnp.concatenate(parts, axis=0))
        pairs.append(jnp.concatenate(tiles[0:pieces:2], axis=1))
        pairs.append(jnp.concatenate(tiles[1:pieces:2], axis=1))
        last.append(tiles[pieces])
    second = jnp.dot(
        jnp.concatenate(stacked, axis=1),
        jnp.concatenate(last, axis=0),
        preferred_element_type=jnp.float32,
    )
    first = jnp.dot(
        jnp.concatenate(sides, axis=1),
        jnp.concatenate(pairs, axis=0),
        preferred_element_type=jnp.float32,
    )
    sums = [None] * (2 * pieces)
    for i in range(pieces):
        sums[i] = second[i * rows : (i + 1) * rows]
    for column in range(pieces // 2):
        for i in range(pieces + 1):
            part = first[i * rows : (i + 1) * rows, column * LANES : (column + 1) * LANES]
            chunk = i - 1 + pieces - 2 * column
            sums[chunk] = part if sums[chunk] is None else sums[chunk] + part
    return sums


def correlate_kernel(units, merged_here, block_ref, moved_ref, *refs):
    if merged_here:
        own_ref, next_ref, out_hbm, out_ref, sems, after_ref, spread_ref = refs
        segments, _, sample_count = own_ref.shape[1:]
    else:
        merged_ref, out_hbm, out_ref, sems = refs
        segments, _, sample_count = merged_ref.shape[1:]
    factor = 1.0 / math.sqrt(sample_count * segments)
    if merged_here:
        merge_in_kernel(next_ref, after_ref, spread_ref, units)
    every = []
    for pair in range(PAIR_DEV):
        block = block_ref[pair]
        if merged_here:
            ahead = block >= NEAR // 2
            place = block % (NEAR // 2)
            receivers = [
                jnp.where(ahead, after_ref[place, i], own_ref[place, i]) for i in range(segments)
            ]
        else:
            receivers = [merged_ref[block, i] for i in range(segments)]
        moved = [moved_ref[pair * segments + i] for i in range(segments)]
        every.append(lag_products(receivers, moved))
    chunks, places, _ = out_ref.shape
    owned = places // PAIR_DEV
    copies = []
    for chunk in range(chunks):
        for pair in range(PAIR_DEV):
            out_ref[chunk, pl.ds(pair, owned, stride=PAIR_DEV), :] = every[pair][chunk] * factor
        copy = pltpu.make_async_copy(
            out_ref.at[chunk].reshape(owned, PAIR_DEV, LANES),
            out_hbm.at[:, :, chunk * LANES : (chunk + 1) * LANES],
            sems.at[chunk],
        )
        copy.start()
        copies.append(copy)
    for copy in copies:
        copy.wait()


def correlate(chosen, toeplitz, receivers, owned, units):
    merged_here = len(receivers) == 2
    shape = (owned, PAIR_DEV, 2 * MAX_LAG)
    chunks = 2 * MAX_LAG // LANES

    def body(*refs):
        correlate_kernel(units, merged_here, *refs)

    scratch = [
        pltpu.VMEM((chunks, owned * PAIR_DEV, LANES), jnp.float32),
        pltpu.SemaphoreType.DMA((chunks,)),
    ]
    if merged_here:
        own = receivers[0]
        scratch.append(pltpu.VMEM(own.shape, own.dtype))
        scratch.append(spread_like(own.shape[1], own.shape[3], units))
    return pl.pallas_call(
        body,
        out_shape=jax.ShapeDtypeStruct(shape, jnp.float32),
        in_specs=[pl.BlockSpec(memory_space=pltpu.SMEM)]
        + [pl.BlockSpec(memory_space=pltpu.VMEM)] * (1 + len(receivers)),
        out_specs=pl.BlockSpec(memory_space=pl.ANY),
        scratch_shapes=scratch,
        compiler_params=pltpu.CompilerParams(vmem_limit_bytes=KERNEL_VMEM),
        name="correlate",
    )(in_scalar(chosen), near_core(toeplitz), *map(near_core, receivers))


def local(recordings, gap_start, dropout_extent, filter_taps, source_channel, receiver_block):
    round_count, sample_count = recordings.shape[1], recordings.shape[3]
    segments = lax.axis_size("tm")
    units = lax.axis_size("chan")
    groups = units
    blocks = round_count * units // BLOCK
    near = blocks // groups
    owned = BLOCK // segments
    rounds_block = BLOCK // units
    slots = min(segments, rounds_block)
    kept = rounds_block // slots
    small = [x.reshape(1, x.size) for x in (filter_taps, gap_start, dropout_extent)]
    small += [source_channel, receiver_block]
    normalized, channels, chosen = normalize(recordings, small, blocks, slots, kept)
    sent = normalized.reshape(slots, groups, near * kept, sample_count)
    sent = jnp.repeat(sent, segments // slots, axis=0) if segments > slots else sent
    got = lax.all_to_all(
        sent.reshape(segments * groups, near * kept, sample_count),
        ("tm", "chan"),
        split_axis=0,
        concat_axis=0,
        tiled=True,
    )
    following = lax.ppermute(got, "chan", [(group, group - 1) for group in range(1, groups)])
    picked = pick_sources(channels, got, units, kept, segments)
    sources = lax.all_gather(picked, "tm")
    if kept == 4 and owned == 4 * units and near == 2:
        toeplitz, own = prepare(channels, sources, (got,), owned, units)
        return correlate(chosen, toeplitz, (own, following), owned, units)
    across = owned // kept
    first = lax.axis_index("tm") * owned % units
    apart = [x.reshape(segments, units, near, kept, sample_count) for x in (got, following)]
    apart = lax.dynamic_slice_in_dim(jnp.concatenate(apart, axis=2), first, across, axis=1)
    merged = apart.transpose(2, 0, 3, 1, 4).reshape(2 * near, segments, owned, sample_count)
    (toeplitz,) = prepare(channels, sources, (), owned, units)
    return correlate(chosen, toeplitz, (merged,), owned, units)


def solution(mesh):
    return jax.shard_map(
        local,
        mesh=mesh,
        in_specs=(
            P("tm", None, "chan", None),
            P("tm", None, "chan"),
            P("tm", None, "chan"),
            P(),
            P("chan"),
            P("chan"),
        ),
        out_specs=P("tm", "chan", None),
        check_vma=False,
    )
```
